128 devices in a mesh: gx: 16 (over z, x), gy: 8 (over y, core).
Axes of the slice: x: 4, y: 4, z: 4, core: 2. Of those that a mesh axis runs over, the one named last changes fastest.
Arguments:
- field: float32 [32, 1024, 1024], P(None, 'gx', 'gy'), may hold values from -6 to 6
- conductivity: float32 [32, 1024, 1024], P(None, 'gx', 'gy'), may hold values from 0.2 to 1
- rate: float32 [32, 1024, 1024], P(None, 'gx', 'gy'), may hold values from 0.05 to 0.5
- patch_cell: int32 [32768], P(('gx', 'gy')), may hold values from 0 to 255
- trainer: int32 [32768, 1], P(('gx', 'gy')), may hold values from 0 to 127; in each aligned block of 256 rows (0 to 255, 256 to 511, ...) at most 4 rows name the same one
- res_slot: int32 [131072], P(('gx', 'gy')), may hold values from 0 to 2047
- reservoir: bfloat16 [262144, 2048], P(('gx', 'gy')), may hold values from -6 to 6
- weights: float32 [2, 1024, 1024], P(None, ('gx', 'gy')), may hold values from -0.1875 to 0.1875
- w_mom: float32 [2, 1024, 1024], P(None, ('gx', 'gy')), may hold values from -0.75 to 0.75
- w_var: float32 [2, 1024, 1024], P(None, ('gx', 'gy')), may hold values from 0.001 to 0.1
- biases: float32 [2, 1024], P(None, ('gx', 'gy')), may hold values from -6 to 6
- b_mom: float32 [2, 1024], P(None, ('gx', 'gy')), may hold values from -0.75 to 0.75
- b_var: float32 [2, 1024], P(None, ('gx', 'gy')), may hold values from 0.001 to 2
Outputs:
- new_field: float32 [32, 1024, 1024], P(None, 'gx', 'gy')
- new_weights: float32 [2, 1024, 1024], P(None, ('gx', 'gy'))
- new_w_mom: float32 [2, 1024, 1024], P(None, ('gx', 'gy'))
- new_w_var: float32 [2, 1024, 1024], P(None, ('gx', 'gy'))
- new_biases: float32 [2, 1024], P(None, ('gx', 'gy'))
- new_b_mom: float32 [2, 1024], P(None, ('gx', 'gy'))
- new_b_var: float32 [2, 1024], P(None, ('gx', 'gy'))
The draws below stay inside these ranges and needn't reach their ends.
Inputs may be any that keep to these rules, and one draw needn't show every extreme that they name: At most 4 of the patches of one device go to one trainer. `res_slot`: slots of the trainer's own reservoir.
All inputs are finite; a program needn't handle non-finite values.
Results may differ from the reference program's by a relative error of at most 0.0003.
The reference program's roundings to bfloat16 on the way count: a program that leaves them out, or rounds other values in their place, can miss the bound.
Values may be sent and summed in bfloat16 or wider, within the bound.
No kernel may reach another device: no remote copies, remote signals or barrier semaphores. Data moves between devices by JAX's collectives and lax.ppermute only.
A program may use at most 128 MiB of HBM per device.

```python
import math
import jax
import jax.numpy as jnp
import numpy as np
from jax import lax

CX = 64
CY = 128
NZ = 32
PW = 32
STEPS = 4
FEAT = 1024
P_DEV = 256
B_OLD = 1024
RES = 2048
CAP = 4
NX = 1024
NY = 1024
N_GX = 16
N_GY = 8


def place_ends(values, own_key, smallest, top_value):
    extent = values.shape
    place = [jax.random.randint(jax.random.fold_in(own_key, axis), (), 0, extent[axis]) for axis in range(len(extent))]
    values = values.at[tuple(place)].set(smallest)
    longest = extent.index(max(extent))
    place[longest] = (place[longest] + 1) % extent[longest]
    return values.at[tuple(place)].set(top_value)


def block_levels(rng, extent, cuts, low, high):
    def one(dim, parts):
        draws = jax.random.uniform(jax.random.fold_in(jax.random.fold_in(rng, 6), dim), (parts,), jnp.float32, low / len(cuts), high / len(cuts))
        return jnp.repeat(jnp.exp(draws), extent[dim] // parts).reshape((-1,) + (1,) * (len(extent) - dim - 1))

    level = one(*cuts[0])
    for cut in cuts[1:]:
        level = level * one(*cut)
    return level


def routed_block(stream_key, own, number, rows, count, top, most, slope):
    order = jax.random.permutation(stream_key, count)
    packed, common = load_shares(count, rows * top, most, slope, True), load_shares(count, rows * top, most, slope, False)
    places = jnp.arange(count)

    def named(sizes, rotation):
        used = int((sizes > 0).sum())
        fixed = max(1, used // 4)
        moved = fixed + (places - fixed + rotation * (used - fixed)) % max(1, count - fixed)
        return jnp.zeros((count,), jnp.int32).at[order[jnp.where(places < fixed, places, moved)]].set(jnp.asarray(sizes, jnp.int32))

    sizes = jnp.where(number % 4 == 0, named(packed, number // 4), named(common, number - number // 4 - 1))
    mixed = jax.random.permutation(jax.random.fold_in(own, 3), count)
    giver, sink = mixed[0:count // 2 * 2:2], mixed[1:count // 2 * 2:2]
    room = jnp.minimum(sizes[giver] - 1, most - sizes[sink]) // 2
    room = jnp.where((giver == order[0]) | (sink == order[0]) | (sizes[sink] == 0), 0, jnp.maximum(room, 0))
    moved = jax.random.randint(jax.random.fold_in(own, 4), (count // 2,), 0, 1 << 20) % (room + 1)
    sizes = sizes.at[giver].add(-moved).at[sink].add(moved)
    labels = jnp.searchsorted(jnp.cumsum(sizes), jnp.arange(rows * top), side="right").astype(jnp.int32)
    table = labels.reshape(top, rows).T
    table = table[jax.random.permutation(jax.random.fold_in(own, 1), rows)]
    rotation = jax.random.randint(jax.random.fold_in(own, 2), (rows, 1), 0, top)
    return jnp.take_along_axis(table, (jnp.arange(top)[None, :] + rotation) % top, axis=1)


def load_shares(number_of, total, bound, lean, full):
    portions = [(1 << 20) // math.isqrt(rank ** lean) + 1 for rank in range(1, number_of + 1)]
    largest = bound if full else min(bound, max(-(-total // number_of), total * portions[0] // sum(portions)))
    least = 1 if total - largest >= number_of - 1 else 0
    holding, spare = [largest] + [least] * (number_of - 1), total - largest - least * (number_of - 1)
    while spare > 0:
        movable = [i for i in range(1, number_of) if holding[i] < largest] or [i for i in range(1, number_of) if holding[i] < bound]
        pool, budget = sum([portions[i] for i in movable]), spare
        for i in movable:
            extra = min(bound - holding[i], max(1, budget * portions[i] // pool), spare)
            holding[i] = holding[i] + extra
            spare = spare - extra
    return np.array(holding)


def bell_draw(stream_key, dims, scale, reach, split=(), held_as=jnp.bfloat16):
    result = jax.random.normal(stream_key, dims, jnp.float32) * scale
    if len(split) > 0:
        result = block_levels(stream_key, dims, split, -0.22, 0.18) * result
    return jnp.clip(result, min=-reach, max=reach).astype(held_as)


def setup_inputs(seed: int = 0) -> dict:
    splits = jax.random.split(jax.random.key(seed), 14)
    field = bell_draw(splits[0], (NZ, NX, NY), 1.0, 6.0, ((1, 16), (2, 8)), jnp.float32)
    conductivity = jnp.clip(0.2 + 0.8 * jax.random.uniform(splits[1], (NZ, NX, NY), jnp.float32) ** block_levels(splits[1], (NZ, NX, NY), ((1, 16), (2, 8)), -0.2, 0.2), 0.2, 1.0)
    rate = jnp.clip(jnp.exp(math.log(0.5) - 2.3025851 * jax.random.uniform(splits[2], (NZ, NX, NY), jnp.float32) ** block_levels(splits[2], (NZ, NX, NY), ((1, 16), (2, 8)), -0.2, 0.2)), 0.05, 0.5)
    patch_cell = place_ends(jax.random.randint(splits[3], (N_GX * N_GY * P_DEV,), 0, CX * CY // PW), jax.random.fold_in(splits[3], 1), 0, (CX * CY // PW) - 1).astype(jnp.int32)
    trainer_keys = jax.random.split(jax.random.fold_in(splits[4], 1), (N_GX * N_GY * P_DEV) // P_DEV)
    trainer_turns = jax.random.permutation(jax.random.fold_in(splits[4], 3), (N_GX * N_GY * P_DEV) // P_DEV)
    trainer = jax.vmap(lambda own, number: routed_block(jax.random.fold_in(splits[4], 2), own, number, P_DEV, N_GX * N_GY, 1, CAP, 2))(trainer_keys, trainer_turns).reshape((N_GX * N_GY * P_DEV, 1))
    res_slot = place_ends(jax.random.randint(splits[5], (N_GX * N_GY * B_OLD,), 0, RES), jax.random.fold_in(splits[5], 1), 0, RES - 1).astype(jnp.int32)
    reservoir = bell_draw(splits[6], (N_GX * N_GY * RES, 2 * FEAT), 1.0, 6.0, ((0, 128),))
    weights = bell_draw(splits[7], (2, FEAT, FEAT), FEAT ** -0.5, 0.1875, ((1, 128),), jnp.float32)
    w_mom = bell_draw(splits[8], (2, FEAT, FEAT), 0.05, 0.75, ((1, 128),), jnp.float32)
    w_var = jnp.clip(jnp.exp(math.log(0.1) - 4.6051702 * jax.random.uniform(splits[9], (2, FEAT, FEAT), jnp.float32) ** block_levels(splits[9], (2, FEAT, FEAT), ((1, 128),), -0.2, 0.2)), 0.001, 0.1)
    biases = bell_draw(splits[10], (2, FEAT), 0.5, 6.0, ((1, 128),), jnp.float32)
    b_mom = bell_draw(splits[11], (2, FEAT), 0.05, 0.75, ((1, 128),), jnp.float32)
    b_var = jnp.clip(jnp.exp(math.log(2.0) - 7.6009024 * jax.random.uniform(splits[12], (2, FEAT), jnp.float32) ** block_levels(splits[12], (2, FEAT), ((1, 128),), -0.2, 0.2)), 0.001, 2.0)
    return dict(field=field, conductivity=conductivity, rate=rate, patch_cell=patch_cell, trainer=trainer, res_slot=res_slot, reservoir=reservoir, weights=weights, w_mom=w_mom, w_var=w_var, biases=biases, b_mom=b_mom, b_var=b_var)


time_step = 0.15
learn_rate = 0.001
beta_one = 0.9
beta_two = 0.99
adam_count = 20
tiny_eps = 1e-08

def update(padded, kpad, rate_inner):
    inner = slice(1, -1)
    centre = padded[1:-1, 1:-1, 1:-1]
    kcentre = kpad[1:-1, 1:-1, 1:-1]
    sides = [(slice(2, None), inner, inner), (slice(None, -2), inner, inner), (inner, slice(2, None), inner), (inner, slice(None, -2), inner), (inner, inner, slice(2, None)), (inner, inner, slice(None, -2))]
    flux = jnp.zeros_like(centre)
    for where in sides:
        flux = flux + 0.5 * (kcentre + kpad[where]) * (padded[where] - centre)
    return centre + time_step * (flux - rate_inner * centre)

def local_grads(rows, live, wbf, bbf):
    width = wbf.shape[1]
    inputs = rows[:, :width]
    target = rows[:, width:].astype(jnp.float32)
    pre = jnp.dot(inputs, wbf[0], preferred_element_type=jnp.float32) + bbf[0].astype(jnp.float32)
    hidden = jnp.tanh(pre)
    hidden_b = hidden.astype(jnp.bfloat16)
    pred = jnp.dot(hidden_b, wbf[1], preferred_element_type=jnp.float32) + bbf[1].astype(jnp.float32)
    count = jnp.sum(live)
    grad_pred = 2.0 * (pred - target) * live[:, None] / count
    grad_pred_b = grad_pred.astype(jnp.bfloat16)
    grad_w2 = jnp.dot(hidden_b.T, grad_pred_b, preferred_element_type=jnp.float32)
    grad_hid = jnp.dot(grad_pred_b, wbf[1].T, preferred_element_type=jnp.float32)
    grad_pre = grad_hid * (1.0 - hidden * hidden)
    grad_pre_b = grad_pre.astype(jnp.bfloat16)
    grad_w1 = jnp.dot(inputs.T, grad_pre_b, preferred_element_type=jnp.float32)
    return (jnp.stack([grad_w1, grad_w2]), jnp.stack([lax.optimization_barrier(jnp.sum(grad_pre, 0)), lax.optimization_barrier(jnp.sum(grad_pred, 0))]))

def adam(param, moment, second, grad):
    moment_new = beta_one * moment + (1.0 - beta_one) * grad
    second_new = beta_two * second + (1.0 - beta_two) * grad * grad
    mhat = moment_new / (1.0 - beta_one ** adam_count)
    vhat = second_new / (1.0 - beta_two ** adam_count)
    return (param - learn_rate * mhat / (jnp.sqrt(vhat) + tiny_eps), moment_new, second_new)

def reference(field, conductivity, rate, patch_cell, trainer, res_slot, reservoir, weights, w_mom, w_var, biases, b_mom, b_var):
    kpad = jnp.pad(conductivity, 1)
    state = field
    for step in range(STEPS):
        state = update(jnp.pad(state, 1), kpad, rate)
    devices = N_GX * N_GY
    cap = max(2, 2 * P_DEV // devices)
    blocks_y = CY // PW
    total = devices * P_DEV
    gidx = jnp.arange(total, dtype=jnp.int32)
    owner = gidx // P_DEV
    xcell = owner // N_GY * CX + patch_cell // blocks_y
    yblock = owner % N_GY * blocks_y + patch_cell % blocks_y
    stacked = jnp.stack([field, state]).reshape(2, NZ, NX, NY // PW, PW)
    picked = stacked[:, :, xcell, yblock, :]
    patches = jnp.transpose(picked, (2, 0, 1, 3)).reshape(total, 2 * FEAT).astype(jnp.bfloat16)
    target_of = trainer[:, 0]
    onehot = (target_of[:, None] == jnp.arange(devices, dtype=jnp.int32)[None, :]).astype(jnp.int32)
    onehot = onehot.reshape(devices, P_DEV, devices)
    rank = (lax.optimization_barrier(jnp.sum(jnp.cumsum(onehot, 1) * onehot, -1)) - 1).reshape(total)
    dest = (target_of * (devices * cap) + owner * cap + rank).astype(jnp.int32)
    inbox = jnp.zeros((devices * devices * cap, 2 * FEAT), jnp.bfloat16).at[dest].set(patches)
    inbox = inbox.reshape(devices, devices * cap, 2 * FEAT)
    alive = jnp.zeros((devices * devices * cap,), jnp.float32).at[dest].set(1.0).reshape(devices, devices * cap)
    wbf = weights.astype(jnp.bfloat16)
    bbf = biases.astype(jnp.bfloat16)

    def one_trainer(carry, which):
        slots = lax.dynamic_slice_in_dim(res_slot, which * B_OLD, B_OLD)
        store = lax.dynamic_slice_in_dim(reservoir, which * RES, RES, 0)
        rows = jnp.concatenate([store[slots], inbox[which]], 0)
        live = jnp.concatenate([jnp.ones((B_OLD,), jnp.float32), alive[which]])
        grad_w, grad_b = local_grads(rows, live, wbf, bbf)
        return ((carry[0] + grad_w, carry[1] + grad_b), None)
    start = (jnp.zeros(weights.shape, jnp.float32), jnp.zeros(biases.shape, jnp.float32))
    (grad_w, grad_b), unused = lax.scan(one_trainer, start, jnp.arange(devices, dtype=jnp.int32))
    new_w, new_wm, new_wv = adam(weights, w_mom, w_var, grad_w)
    new_b, new_bm, new_bv = adam(biases, b_mom, b_var, grad_b)
    return (state, new_w, new_wm, new_wv, new_b, new_bm, new_bv)
```

```python
import jax
import jax.numpy as jnp
from jax import lax
from jax.sharding import PartitionSpec as P

PW = 32
STEPS = 4
AXES = ("gx", "gy")

time_step = 0.15
learn_rate = 0.001
beta_one = 0.9
beta_two = 0.99
adam_count = 20
tiny_eps = 1e-08


def with_halo(x, sides, width):
    for axis, dim in sides:
        peers, length = (lax.axis_size(axis), x.shape[dim])
        up = [(i, (i + 1) % peers) for i in range(peers - 1)]
        down = [(j, i) for i, j in up]
        last = lax.slice_in_dim(x, length - width, length, axis=dim)
        first = lax.slice_in_dim(x, 0, width, axis=dim)
        before = lax.ppermute(last, axis, up)
        after = lax.ppermute(first, axis, down)
        x = jnp.concatenate([before, x, after], axis=dim)
    return x


def update(padded, kpad, rate_inner):
    inner = slice(1, -1)
    centre = padded[1:-1, 1:-1, 1:-1]
    kcentre = kpad[1:-1, 1:-1, 1:-1]
    sides = [
        (slice(2, None), inner, inner),
        (slice(None, -2), inner, inner),
        (inner, slice(2, None), inner),
        (inner, slice(None, -2), inner),
        (inner, inner, slice(2, None)),
        (inner, inner, slice(None, -2)),
    ]
    flux = jnp.zeros_like(centre)
    for where in sides:
        flux = flux + 0.5 * (kcentre + kpad[where]) * (padded[where] - centre)
    return centre + time_step * (flux - rate_inner * centre)


def zpad(array):
    return jnp.pad(array, ((1, 1), (0, 0), (0, 0)))


def adam(param, moment, second, grad):
    moment_new = beta_one * moment + (1.0 - beta_one) * grad
    second_new = beta_two * second + (1.0 - beta_two) * grad * grad
    mhat = moment_new / (1.0 - beta_one**adam_count)
    vhat = second_new / (1.0 - beta_two**adam_count)
    return (param - learn_rate * mhat / (jnp.sqrt(vhat) + tiny_eps), moment_new, second_new)


def chip_groups(devices):
    return [list(range(core, devices, 2)) for core in range(2)]


def swap_cores(x, devices):
    return lax.ppermute(x, AXES, [(d, d ^ 1) for d in range(devices)])


def chips_all_to_all(x, devices):
    return lax.all_to_all(
        x, AXES, 0, 0, tiled=True, axis_index_groups=chip_groups(devices)
    )


def gather_params(weights, biases, hist, core, devices):
    chips = devices // 2
    layers, own, width = weights.shape
    extra = jnp.zeros((layers, own, devices), jnp.bfloat16)
    extra = extra.at[0, 0, :].set(hist.astype(jnp.bfloat16))
    extra = extra.at[:, 1, :own].set(biases.astype(jnp.bfloat16))
    pay = jnp.concatenate([weights.astype(jnp.bfloat16), extra], -1)
    got = chips_all_to_all(jnp.broadcast_to(pay[None], (chips,) + pay.shape), devices)
    other = swap_cores(got, devices)
    first = jnp.where(core == 0, got, other)
    second = jnp.where(core == 0, other, got)
    both = jnp.stack([first, second], 1).transpose(2, 0, 1, 3, 4)
    full = both.reshape(layers, devices * own, width + devices)
    tail = full[:, :, width:].reshape(layers, devices, own, devices)
    counts = jnp.sum(tail[0, :, 0, :].astype(jnp.float32), 0)
    bfull = tail[:, :, 1, :own].reshape(layers, devices * own).astype(jnp.float32)
    return full[:, :, :width], bfull, counts


def chunks(grad, devices):
    rows, width = grad.shape
    own = rows // devices
    tiles = width // 128
    grad = grad.reshape(devices // 2, 2, own, tiles, 128)
    return grad.transpose(1, 0, 3, 2, 4).reshape(2, devices // 2, tiles * own, 128)


def unchunk(share, own, width):
    return share.reshape(width // 128, own, 128).transpose(1, 0, 2).reshape(own, width)


def reduce_chunks(parts, core, devices):
    mine = lax.dynamic_index_in_dim(parts, core, 0, keepdims=False)
    theirs = lax.dynamic_index_in_dim(parts, 1 - core, 0, keepdims=False)
    mine = mine + swap_cores(theirs, devices)
    return jnp.sum(chips_all_to_all(mine, devices), 0)


def local(
    field,
    conductivity,
    rate,
    patch_cell,
    trainer,
    res_slot,
    reservoir,
    weights,
    w_mom,
    w_var,
    biases,
    b_mom,
    b_var,
):
    depth, cells_x, cells_y = field.shape
    devices = lax.axis_size("gx") * lax.axis_size("gy")
    me = lax.axis_index(AXES)
    core = me & 1
    own, width = weights.shape[1:]
    ids = jnp.arange(devices, dtype=jnp.int32)
    onehot = trainer == ids[None, :]
    hist = jnp.sum(onehot.astype(jnp.float32), 0)
    wfull, bfull, counts = gather_params(weights, biases, hist, core, devices)

    state = field
    kpad = zpad(with_halo(conductivity, (("gx", 1), ("gy", 2)), 1))
    for step in range(STEPS):
        padded = with_halo(state, (("gx", 1), ("gy", 2)), 1)
        state = update(zpad(padded), kpad, rate)
    count_dev = patch_cell.shape[0]
    stacked = jnp.stack([field, state]).astype(jnp.bfloat16)
    table = stacked.reshape(2, depth, cells_x, cells_y // PW, PW).transpose(2, 3, 0, 1, 4)
    table = table.reshape(cells_x * cells_y // PW, 2 * depth * PW)
    pick = patch_cell[:, None] == jnp.arange(table.shape[0], dtype=jnp.int32)[None, :]
    patches = jnp.dot(pick.astype(jnp.bfloat16), table, preferred_element_type=jnp.float32)
    patches = patches.astype(jnp.bfloat16)

    old = res_slot.shape[0]
    sizes = old + counts
    own_size = jnp.sum(jnp.where(ids == me, sizes, 0.0))
    new_size = jnp.sum(jnp.where(onehot, sizes[None, :], 0.0), 1)
    sizes_of = jnp.concatenate([jnp.broadcast_to(own_size, (old,)), new_size])[:, None]
    rows = jnp.concatenate([reservoir[res_slot], patches], 0)

    inputs = rows[:, :width]
    target = rows[:, width:].astype(jnp.float32)
    pre = jnp.dot(inputs, wfull[0], preferred_element_type=jnp.float32) + bfull[0]
    hidden = jnp.tanh(pre)
    hidden_b = hidden.astype(jnp.bfloat16)
    pred = jnp.dot(hidden_b, wfull[1], preferred_element_type=jnp.float32) + bfull[1]
    grad_pred = 2.0 * (pred - target) / sizes_of
    grad_pred_b = grad_pred.astype(jnp.bfloat16)
    grad_w2 = jnp.dot(hidden_b.T, grad_pred_b, preferred_element_type=jnp.float32)
    share_w2 = reduce_chunks(chunks(grad_w2, devices), core, devices)
    grad_hid = jnp.dot(grad_pred_b, wfull[1].T, preferred_element_type=jnp.float32)
    grad_pre = grad_hid * (1.0 - hidden * hidden)
    grad_pre_b = grad_pre.astype(jnp.bfloat16)
    grad_w1 = jnp.dot(inputs.T, grad_pre_b, preferred_element_type=jnp.float32)
    grad_b = jnp.stack([jnp.sum(grad_pre, 0), jnp.sum(grad_pred, 0)])
    tile_b = grad_b.reshape(2, devices // 2, 2, own).transpose(2, 1, 0, 3)
    tile_b = jnp.pad(tile_b, ((0, 0), (0, 0), (0, 8 - 2), (0, 128 - own)))
    parts = jnp.concatenate([chunks(grad_w1, devices), tile_b], 2)
    share_w1 = reduce_chunks(parts, core, devices)
    share_w = jnp.stack(
        [unchunk(share_w1[: own * width // 128], own, width), unchunk(share_w2, own, width)]
    )
    share_b = share_w1[own * width // 128 :][:2, :own]
    new_w, new_wm, new_wv = adam(weights, w_mom, w_var, share_w)
    new_b, new_bm, new_bv = adam(biases, b_mom, b_var, share_b)
    return (state, new_w, new_wm, new_wv, new_b, new_bm, new_bv)


def solution(mesh):
    return jax.shard_map(
        local,
        mesh=mesh,
        in_specs=(
            P(None, "gx", "gy"),
            P(None, "gx", "gy"),
            P(None, "gx", "gy"),
            P(("gx", "gy")),
            P(("gx", "gy"), None),
            P(("gx", "gy")),
            P(("gx", "gy"), None),
            P(None, ("gx", "gy"), None),
            P(None, ("gx", "gy"), None),
            P(None, ("gx", "gy"), None),
            P(None, ("gx", "gy")),
            P(None, ("gx", "gy")),
            P(None, ("gx", "gy")),
        ),
        out_specs=(
            P(None, "gx", "gy"),
            P(None, ("gx", "gy"), None),
            P(None, ("gx", "gy"), None),
            P(None, ("gx", "gy"), None),
            P(None, ("gx", "gy")),
            P(None, ("gx", "gy")),
            P(None, ("gx", "gy")),
        ),
        check_vma=False,
    )
```

```python
import jax
import jax.numpy as jnp
from jax import lax
from jax.experimental import pallas as pl
from jax.experimental.pallas import tpu as pltpu
from jax.sharding import PartitionSpec as P


PW = 32
STEPS = 4
AXES = ("gx", "gy")

time_step = 0.15
learn_rate = 0.001
beta_one = 0.9
beta_two = 0.99
adam_count = 20
tiny_eps = 1e-08


def shift_pairs(axis):
    peers = lax.axis_size(axis)
    up = [(i, i + 1) for i in range(peers - 1)]
    return up, [(j, i) for i, j in up]


def exchange(first, last, axis):
    up, down = shift_pairs(axis)
    return lax.ppermute(first, axis, down), lax.ppermute(last, axis, up)


def lane_ids(shape):
    return lax.broadcasted_iota(jnp.int32, shape, len(shape) - 1)


def pack_kernel(u_ref, k_ref, r_ref, halo_ref, first_ref, last_ref):
    depth = u_ref.shape[0]
    slot = lane_ids((1, 128)) // STEPS
    for a, ref in enumerate((u_ref, k_ref, r_ref)):
        for part, rows in (("main", ref.shape[1]), ("halo", 2 * STEPS)):
            first = jnp.zeros((rows, 128), jnp.float32)
            last = first
            for z in range(depth):
                slab = ref[z] if part == "main" else halo_ref[a, z]
                turned = pltpu.roll(slab, z * STEPS, 1) if z else slab
                first = jnp.where(slot == z, turned, first)
                last = jnp.where(slot == (z - 1) % depth, turned, last)
            at = slice(0, rows) if part == "main" else slice(ref.shape[1], ref.shape[1] + rows)
            first_ref[a, at, :] = first
            last_ref[a, at, :] = last


def pack_sides(field, conductivity, rate, halo):
    rows = field.shape[1] + 2 * STEPS
    out = jax.ShapeDtypeStruct((3, rows, 128), jnp.float32)
    return pl.pallas_call(pack_kernel, out_shape=(out, out), name="pack_sides", cost_estimate=pl.CostEstimate(flops=1 << 24, bytes_accessed=12 << 20, transcendentals=0))(
        field, conductivity, rate, halo
    )


def table_rows(read, table_ref, level, depth):
    group = lane_ids((1, 128)) // PW
    per = 128 // PW

    def body(block, carry):
        slabs = [read(block * per + k) for k in range(per)]
        cells_x = slabs[0].shape[0]
        for yb in range(per):
            row = None
            for k in range(per):
                turn = (k - yb) % per * PW
                part = pltpu.roll(slabs[k], turn, 1) if turn else slabs[k]
                row = part if row is None else jnp.where(group == k, part, row)
            at = pl.multiple_of(level * depth * PW + block * 128, 128)
            table_ref[yb * cells_x : (yb + 1) * cells_x, pl.ds(at, 128)] = row.astype(jnp.bfloat16)
        return carry

    lax.fori_loop(0, depth // per, body, 0)


def solve_kernel(
    pos_ref,
    u_ref,
    k_ref,
    r_ref,
    halo_ref,
    right_ref,
    left_ref,
    out_ref,
    table_ref,
    ua,
    ub,
    kk,
    rr,
    cx,
    cy,
    cz,
    dt_ref,
):
    depth, cells_x, cells_y = u_ref.shape
    rows, lanes = cells_x + 2 * STEPS, 2 * cells_y
    lane = lane_ids((1, cells_y))
    blank = jnp.zeros((rows, lanes), jnp.float32)
    for ref in (ua, ub, kk):
        ref[0] = blank
        ref[depth + 1] = blank
    for z in range(depth):
        for a, (src, dst, at) in enumerate(((u_ref, ua, z + 1), (k_ref, kk, z + 1), (r_ref, rr, z))):
            dst[at, 0:cells_x, 0:cells_y] = src[z]
            dst[at, cells_x:rows, 0:cells_y] = halo_ref[a, z]
            turn = -z * STEPS % cells_y
            right, left = right_ref[a], left_ref[a]
            if turn:
                right, left = pltpu.roll(right, turn, 1), pltpu.roll(left, turn, 1)
            side = jnp.where(lane < STEPS, right, 0.0)
            side = jnp.where(lane >= cells_y - STEPS, left, side)
            dst[at, :, cells_y:lanes] = side

    def faces(z, carry):
        k = kk[z + 1]
        cz[z] = 0.5 * (kk[z] + k)
        cx[z] = 0.5 * (k + pltpu.roll(k, rows - 1, 0))
        cy[z] = 0.5 * (k + pltpu.roll(k, lanes - 1, 1))
        return carry

    lax.fori_loop(0, depth, faces, 0)
    cz[depth] = 0.5 * kk[depth]

    gx, gy = pos_ref[0], pos_ref[1]
    row_id = lax.broadcasted_iota(jnp.int32, (rows, lanes), 0)
    lane_id = lax.broadcasted_iota(jnp.int32, (rows, lanes), 1)
    below = jnp.where(gx < pos_ref[2] - 1, 1, 0)
    above = jnp.where(gx > 0, 1, 0)
    after = jnp.where(gy < pos_ref[3] - 1, 1, 0)
    before = jnp.where(gy > 0, 1, 0)
    row_in = jnp.where(row_id < cells_x, 1, jnp.where(row_id < cells_x + STEPS, below, above))
    lane_in = jnp.where(lane_id < cells_y + STEPS, after, 0)
    lane_in = jnp.where(lane_id >= lanes - STEPS, before, lane_in)
    lane_in = jnp.where(lane_id < cells_y, 1, lane_in)
    dt_ref[...] = jnp.where(row_in * lane_in > 0, jnp.float32(time_step), jnp.float32(0.0))

    sub = lax.broadcasted_iota(jnp.int32, (8, cells_y), 0)
    col = lax.broadcasted_iota(jnp.int32, (8, cells_y), 1)
    tiles = rows // 8

    def advance(src, dst, last):
        wide = 1 if last else 2
        inner = cells_x // 8 if last else tiles

        def body(z, carry):
            def at(t, w):
                return slice(8 * t, 8 * t + 8), slice(cells_y * w, cells_y * (w + 1))

            def load(ref, i, t, w):
                r, c = at(t, w)
                return ref[i, r, c]

            u = [[load(src, z + 1, t, w) for w in range(2)] for t in range(tiles)]

            def face_x(t, w):
                here, there = u[t][w], u[(t + 1) % tiles][w]
                turned = jnp.where(
                    sub == 7, pltpu.roll(there, 7, 0), pltpu.roll(here, 7, 0)
                )
                return load(cx, z, t, w) * (turned - here)

            def face_y(t, w):
                here, there = u[t][w], u[t][1 - w]
                turned = jnp.where(
                    col == cells_y - 1,
                    pltpu.roll(there, cells_y - 1, 1),
                    pltpu.roll(here, cells_y - 1, 1),
                )
                return load(cy, z, t, w) * (turned - here)

            before = [pltpu.roll(face_x(tiles - 1, w), 1, 0) for w in range(wide)]
            for t in range(inner):
                ys = [face_y(t, w) for w in range(2)]
                turned_y = [pltpu.roll(y, 1, 1) for y in ys]
                for w in range(wide):
                    here = u[t][w]
                    flux = load(cz, z + 1, t, w) * (load(src, z + 2, t, w) - here)
                    flux = flux + load(cz, z, t, w) * (load(src, z, t, w) - here)
                    side = face_x(t, w)
                    flux = flux + side
                    turned = pltpu.roll(side, 1, 0)
                    flux = flux - jnp.where(sub == 0, before[w], turned)
                    before[w] = turned
                    flux = flux + ys[w]
                    flux = flux - jnp.where(col == 0, turned_y[1 - w], turned_y[w])
                    r, c = at(t, w)
                    loss = flux - load(rr, z, t, w) * here
                    if last:
                        out_ref[z, r, c] = here + time_step * loss
                    elif w == 0 and t < cells_x // 8:
                        dst[z + 1, r, c] = here + time_step * loss
                    else:
                        dst[z + 1, r, c] = here + dt_ref[r, c] * loss
            return carry

        lax.fori_loop(0, depth, body, 0)

    src, dst = ua, ub
    for step in range(STEPS):
        advance(src, dst, step == STEPS - 1)
        src, dst = dst, src
    table_rows(lambda z: u_ref[z], table_ref, 0, depth)
    table_rows(lambda z: out_ref[z], table_ref, 1, depth)


def solve(field, conductivity, rate):
    depth, cells_x, cells_y = field.shape
    rows, lanes = cells_x + 2 * STEPS, 2 * cells_y
    arrays = (field, conductivity, rate)
    first = jnp.stack([x[:, :STEPS] for x in arrays])
    last = jnp.stack([x[:, cells_x - STEPS :] for x in arrays])
    below, above = exchange(first, last, "gx")
    halo = jnp.concatenate([below, above], 2)
    first, last = pack_sides(*arrays, halo)
    right, left = exchange(first, last, "gy")
    pos = [lax.axis_index("gx"), lax.axis_index("gy"), lax.axis_size("gx"), lax.axis_size("gy")]
    pos = jnp.stack([jnp.asarray(p, jnp.int32) for p in pos])
    padded = pltpu.VMEM((depth + 2, rows, lanes), jnp.float32)
    whole = pltpu.VMEM((depth, rows, lanes), jnp.float32)
    cells = cells_x * cells_y // PW
    return pl.pallas_call(
        solve_kernel,
        out_shape=(
            jax.ShapeDtypeStruct(field.shape, jnp.float32),
            jax.ShapeDtypeStruct((cells, 2 * depth * PW), jnp.bfloat16),
        ),
        in_specs=[pl.BlockSpec(memory_space=pltpu.SMEM)]
        + [pl.BlockSpec(memory_space=pltpu.VMEM)] * 6,
        out_specs=(pl.BlockSpec(memory_space=pltpu.VMEM),) * 2,
        scratch_shapes=[padded, padded, padded, whole, whole, whole,
            pltpu.VMEM((depth + 1, rows, lanes), jnp.float32),
            pltpu.VMEM((rows, lanes), jnp.float32)],
        cost_estimate=pl.CostEstimate(
            flops=40 * STEPS * depth * rows * lanes, bytes_accessed=64 << 20, transcendentals=0
        ),
        name="solve",
    )(pos, *arrays, halo, right, left)


def adam(param, moment, second, grad):
    moment_new = beta_one * moment + (1.0 - beta_one) * grad
    second_new = beta_two * second + (1.0 - beta_two) * grad * grad
    mhat = moment_new / (1.0 - beta_one**adam_count)
    vhat = second_new / (1.0 - beta_two**adam_count)
    return (param - learn_rate * mhat / (jnp.sqrt(vhat) + tiny_eps), moment_new, second_new)


def chip_groups(devices):
    return [list(range(core, devices, 2)) for core in range(2)]


def swap_cores(x, devices):
    return lax.ppermute(x, AXES, [(d, d ^ 1) for d in range(devices)])


def chips_all_to_all(x, devices):
    return lax.all_to_all(
        x, AXES, 0, 0, tiled=True, axis_index_groups=chip_groups(devices)
    )


def gather_params(weights, biases, hist, core, devices):
    chips = devices // 2
    layers, own, width = weights.shape
    extra = jnp.zeros((layers, own, devices), jnp.bfloat16)
    extra = extra.at[0, 0, :].set(hist.astype(jnp.bfloat16))
    extra = extra.at[:, 1, :own].set(biases.astype(jnp.bfloat16))
    pay = jnp.concatenate([weights.astype(jnp.bfloat16), extra], -1)
    got = chips_all_to_all(jnp.broadcast_to(pay[None], (chips,) + pay.shape), devices)
    other = swap_cores(got, devices)
    first = jnp.where(core == 0, got, other)
    second = jnp.where(core == 0, other, got)
    both = jnp.stack([first, second], 1).transpose(2, 0, 1, 3, 4)
    full = both.reshape(layers, devices * own, width + devices)
    tail = full[:, :, width:].reshape(layers, devices, own, devices)
    counts = jnp.sum(tail[0, :, 0, :].astype(jnp.float32), 0)
    bfull = tail[:, :, 1, :own].reshape(layers, devices * own).astype(jnp.float32)
    return full[:, :, :width], bfull, counts


def chunks(grad, devices):
    rows, width = grad.shape
    own = rows // devices
    tiles = width // 128
    grad = grad.reshape(devices // 2, 2, own, tiles, 128)
    return grad.transpose(1, 0, 3, 2, 4).reshape(2, devices // 2, tiles * own, 128)


def unchunk(share, own, width):
    return share.reshape(width // 128, own, 128).transpose(1, 0, 2).reshape(own, width)


def reduce_chunks(parts, core, devices):
    mine = lax.dynamic_index_in_dim(parts, core, 0, keepdims=False)
    theirs = lax.dynamic_index_in_dim(parts, 1 - core, 0, keepdims=False)
    theirs = swap_cores(theirs, devices)
    mine = mine + theirs
    return jnp.sum(chips_all_to_all(mine, devices), 0)


def step_all(
    field,
    conductivity,
    rate,
    patch_cell,
    trainer,
    res_slot,
    reservoir,
    weights,
    w_mom,
    w_var,
    biases,
    b_mom,
    b_var,
):
    _, cells_x, cells_y = field.shape
    devices = lax.axis_size("gx") * lax.axis_size("gy")
    me = lax.axis_index(AXES)
    core = me & 1
    own, width = weights.shape[1:]
    ids = jnp.arange(devices, dtype=jnp.int32)
    onehot = trainer == ids[None, :]
    hist = jnp.sum(onehot.astype(jnp.float32), 0)
    wfull, bfull, counts = gather_params(weights, biases, hist, core, devices)

    state, table = solve(field, conductivity, rate)
    blocks = cells_y // PW
    place = patch_cell % blocks * cells_x + patch_cell // blocks
    pick = place[:, None] == jnp.arange(table.shape[0], dtype=jnp.int32)[None, :]
    patches = jnp.dot(pick.astype(jnp.bfloat16), table, preferred_element_type=jnp.float32)
    patches = patches.astype(jnp.bfloat16)

    old = res_slot.shape[0]
    sizes = old + counts
    own_size = jnp.sum(jnp.where(ids == me, sizes, 0.0))
    new_size = jnp.sum(jnp.where(onehot, sizes[None, :], 0.0), 1)
    sizes_of = jnp.concatenate([jnp.broadcast_to(own_size, (old,)), new_size])[:, None]
    stored = reservoir[res_slot]
    rows = jnp.concatenate([stored, patches], 0)

    inputs = rows[:, :width]
    target = rows[:, width:].astype(jnp.float32)
    pre = jnp.dot(inputs, wfull[0], preferred_element_type=jnp.float32) + bfull[0]
    hidden = jnp.tanh(pre)
    hidden_b = hidden.astype(jnp.bfloat16)
    pred = jnp.dot(hidden_b, wfull[1], preferred_element_type=jnp.float32) + bfull[1]
    grad_pred = 2.0 * (pred - target) / sizes_of
    grad_pred_b = grad_pred.astype(jnp.bfloat16)
    grad_w2 = jnp.dot(hidden_b.T, grad_pred_b, preferred_element_type=jnp.float32)
    share_w2 = reduce_chunks(chunks(grad_w2, devices), core, devices)
    grad_hid = jnp.dot(grad_pred_b, wfull[1].T, preferred_element_type=jnp.float32)
    grad_pre = grad_hid * (1.0 - hidden * hidden)
    grad_pre_b = grad_pre.astype(jnp.bfloat16)
    grad_b0 = jnp.sum(grad_pre, 0)
    grad_w1 = jnp.dot(inputs.T, grad_pre_b, preferred_element_type=jnp.float32)
    grad_b = jnp.stack([grad_b0, jnp.sum(grad_pred, 0)])
    tile_b = grad_b.reshape(2, devices // 2, 2, own).transpose(2, 1, 0, 3)
    tile_b = jnp.pad(tile_b, ((0, 0), (0, 0), (0, 8 - 2), (0, 128 - own)))
    parts = jnp.concatenate([chunks(grad_w1, devices), tile_b], 2)
    share_w1 = reduce_chunks(parts, core, devices)
    share_w = jnp.stack(
        [unchunk(share_w1[: own * width // 128], own, width), unchunk(share_w2, own, width)]
    )
    share_b = share_w1[own * width // 128 :][:2, :own]
    new_w, new_wm, new_wv = adam(weights, w_mom, w_var, share_w)
    new_b, new_bm, new_bv = adam(biases, b_mom, b_var, share_b)
    return (state, new_w, new_wm, new_wv, new_b, new_bm, new_bv)


def solution(mesh):
    return jax.shard_map(
        step_all,
        mesh=mesh,
        in_specs=(
            P(None, "gx", "gy"),
            P(None, "gx", "gy"),
            P(None, "gx", "gy"),
            P(("gx", "gy")),
            P(("gx", "gy"), None),
            P(("gx", "gy")),
            P(("gx", "gy"), None),
            P(None, ("gx", "gy"), None),
            P(None, ("gx", "gy"), None),
            P(None, ("gx", "gy"), None),
            P(None, ("gx", "gy")),
            P(None, ("gx", "gy")),
            P(None, ("gx", "gy")),
        ),
        out_specs=(
            P(None, "gx", "gy"),
            P(None, ("gx", "gy"), None),
            P(None, ("gx", "gy"), None),
            P(None, ("gx", "gy"), None),
            P(None, ("gx", "gy")),
            P(None, ("gx", "gy")),
            P(None, ("gx", "gy")),
        ),
        check_vma=False,
    )
```

```python
import jax
import jax.numpy as jnp
from jax import lax
from jax.experimental import pallas as pl
from jax.experimental.pallas import tpu as pltpu
from jax.sharding import PartitionSpec as P


PW = 32
STEPS = 4
AXES = ("gx", "gy")

time_step = 0.15
learn_rate = 0.001
beta_one = 0.9
beta_two = 0.99
adam_count = 20
tiny_eps = 1e-08


def shift_pairs(axis):
    peers = lax.axis_size(axis)
    up = [(i, i + 1) for i in range(peers - 1)]
    return up, [(j, i) for i, j in up]


def exchange(first, last, axis):
    up, down = shift_pairs(axis)
    return lax.ppermute(first, axis, down), lax.ppermute(last, axis, up)


def lane_ids(shape):
    return lax.broadcasted_iota(jnp.int32, shape, len(shape) - 1)


def pack_kernel(u_ref, k_ref, r_ref, halo_ref, first_ref, last_ref):
    depth = u_ref.shape[0]
    slot = lane_ids((1, 128)) // STEPS
    for a, ref in enumerate((u_ref, k_ref, r_ref)):
        for part, rows in (("main", ref.shape[1]), ("halo", 2 * STEPS)):
            first = jnp.zeros((rows, 128), jnp.float32)
            last = first
            for z in range(depth):
                slab = ref[z] if part == "main" else halo_ref[a, z]
                turned = pltpu.roll(slab, z * STEPS, 1) if z else slab
                first = jnp.where(slot == z, turned, first)
                last = jnp.where(slot == (z - 1) % depth, turned, last)
            at = slice(0, rows) if part == "main" else slice(ref.shape[1], ref.shape[1] + rows)
            first_ref[a, at, :] = first
            last_ref[a, at, :] = last


def pack_sides(field, conductivity, rate, halo):
    rows = field.shape[1] + 2 * STEPS
    out = jax.ShapeDtypeStruct((3, rows, 128), jnp.float32)
    return pl.pallas_call(pack_kernel, out_shape=(out, out), name="pack_sides", cost_estimate=pl.CostEstimate(flops=1 << 24, bytes_accessed=12 << 20, transcendentals=0))(
        field, conductivity, rate, halo
    )


def table_rows(read, table_ref, level, depth):
    group = lane_ids((1, 128)) // PW
    per = 128 // PW

    def body(block, carry):
        slabs = [read(block * per + k) for k in range(per)]
        cells_x = slabs[0].shape[0]
        for yb in range(per):
            row = None
            for k in range(per):
                turn = (k - yb) % per * PW
                part = pltpu.roll(slabs[k], turn, 1) if turn else slabs[k]
                row = part if row is None else jnp.where(group == k, part, row)
            at = pl.multiple_of(level * depth * PW + block * 128, 128)
            table_ref[yb * cells_x : (yb + 1) * cells_x, pl.ds(at, 128)] = row.astype(jnp.bfloat16)
        return carry

    lax.fori_loop(0, depth // per, body, 0)


MARGIN = 8


def solve_kernel(
    pos_ref,
    u_ref,
    k_ref,
    r_ref,
    halo_ref,
    right_ref,
    left_ref,
    out_ref,
    table_ref,
    ua,
    ub,
    kk,
    rr,
    cx,
    cy,
    cz,
    dt_ref,
):
    depth, cells_x, cells_y = u_ref.shape
    halo_top, main = MARGIN, 2 * MARGIN
    halo_low, end = main + cells_x, main + cells_x + MARGIN
    lane = lane_ids((1, cells_y))
    sub = lax.broadcasted_iota(jnp.int32, (8, cells_y), 0)
    col = lax.broadcasted_iota(jnp.int32, (8, cells_y), 1)
    blank = jnp.zeros((end + MARGIN, cells_y), jnp.float32)
    edge = jnp.zeros((MARGIN, cells_y), jnp.float32)
    for w in range(2):
        for ref in (ua, ub, kk):
            ref[w, 0] = blank
            ref[w, depth + 1] = blank

    def clear(z, carry):
        for w in range(2):
            for ref in (ua, ub, kk):
                ref[w, z + 1, 0:halo_top, :] = edge
                ref[w, z + 1, end : end + MARGIN, :] = edge
        return carry

    lax.fori_loop(0, depth, clear, 0)

    def place(ref, w, at, body, ends):
        ref[w, at, main:halo_low, :] = body
        ref[w, at, halo_top:main, :] = jnp.where(sub >= STEPS, ends, 0.0)
        ref[w, at, halo_low:end, :] = jnp.where(sub < STEPS, ends, 0.0)

    for z in range(depth):
        for a, (src, dst, at) in enumerate(((u_ref, ua, z + 1), (k_ref, kk, z + 1), (r_ref, rr, z))):
            place(dst, 0, at, src[z], halo_ref[a, z])
            turn = -z * STEPS % cells_y
            side = jnp.where(lane // STEPS == z, right_ref[a], left_ref[a])
            if turn:
                side = pltpu.roll(side, turn, 1)
            place(dst, 1, at, side[:cells_x], side[cells_x:])

    def rows(t, shift=0):
        return slice(8 * t + shift, 8 * t + 8 + shift)

    def turned(pair, back):
        amount = 1 if back else cells_y - 1
        seam = col == (0 if back else cells_y - 1)
        both = [pltpu.roll(x, amount, 1) for x in pair]
        return [jnp.where(seam, both[1 - w], both[w]) for w in range(2)]

    tiles = end // 8
    half = 0.5 * time_step

    def faces(z, carry):
        for t in range(tiles):
            k = [kk[w, z + 1, rows(t), :] for w in range(2)]
            after = turned(k, False)
            for w in range(2):
                cz[w, z, rows(t), :] = half * (kk[w, z, rows(t), :] + k[w])
                cx[w, z, rows(t), :] = half * (k[w] + kk[w, z + 1, rows(t, 1), :])
                cy[w, z, rows(t), :] = half * (k[w] + after[w])
        return carry

    lax.fori_loop(0, depth, faces, 0)
    for w in range(2):
        cz[w, depth] = half * kk[w, depth]

    def keeps(z, carry):
        for t in range(halo_top // 8, tiles):
            ys = [cy[w, z, rows(t), :] for w in range(2)]
            back = turned(ys, True)
            for w in range(2):
                loss = cz[w, z + 1, rows(t), :] + cz[w, z, rows(t), :]
                loss = loss + (cx[w, z, rows(t), :] + cx[w, z, rows(t, -1), :])
                loss = loss + (ys[w] + back[w])
                rr[w, z, rows(t), :] = (1.0 - time_step * rr[w, z, rows(t), :]) - loss
        return carry

    lax.fori_loop(0, depth, keeps, 0)

    gx, gy = pos_ref[0], pos_ref[1]
    below = jnp.where(gx < pos_ref[2] - 1, 1, 0)
    above = jnp.where(gx > 0, 1, 0)
    after = jnp.where(gy < pos_ref[3] - 1, 1, 0)
    before = jnp.where(gy > 0, 1, 0)
    row_id = lax.broadcasted_iota(jnp.int32, blank.shape, 0)
    lane_id = lax.broadcasted_iota(jnp.int32, blank.shape, 1)
    row_in = jnp.where(row_id < main, above, jnp.where(row_id < halo_low, 1, below))
    row_in = jnp.where((row_id < main - STEPS) | (row_id >= halo_low + STEPS), 0, row_in)
    side_in = jnp.where(lane_id < STEPS, after, 0)
    side_in = jnp.where(lane_id >= cells_y - STEPS, before, side_in)
    for w, inside in ((0, row_in), (1, row_in * side_in)):
        dt_ref[w] = jnp.where(inside > 0, jnp.float32(1.0), jnp.float32(0.0))

    def advance(src, dst, last):
        picks = (0,) if last else (0, 1)
        first_tile, end_tile = (main // 8, halo_low // 8) if last else (halo_top // 8, end // 8)

        def body(z, carry):
            for t in range(first_tile, end_tile):
                u = [src[w, z + 1, rows(t), :] for w in range(2)]
                after = turned(u, False)
                ys = [cy[w, z, rows(t), :] for w in range(2)]
                back = turned([ys[w] * u[w] for w in range(2)], True)
                for w in picks:
                    total = cz[w, z + 1, rows(t), :] * src[w, z + 2, rows(t), :]
                    total = total + cz[w, z, rows(t), :] * src[w, z, rows(t), :]
                    total = total + cx[w, z, rows(t), :] * src[w, z + 1, rows(t, 1), :]
                    total = total + cx[w, z, rows(t, -1), :] * src[w, z + 1, rows(t, -1), :]
                    total = total + (ys[w] * after[w] + back[w])
                    total = total + rr[w, z, rows(t), :] * u[w]
                    if last:
                        out_ref[z, rows(t - main // 8), :] = total
                    elif w == 0 and main <= 8 * t < halo_low:
                        dst[w, z + 1, rows(t), :] = total
                    else:
                        dst[w, z + 1, rows(t), :] = dt_ref[w, rows(t), :] * total
            return carry

        lax.fori_loop(0, depth, body, 0)

    src, dst = ua, ub
    for step in range(STEPS):
        advance(src, dst, step == STEPS - 1)
        src, dst = dst, src
    table_rows(lambda z: u_ref[z], table_ref, 0, depth)
    table_rows(lambda z: out_ref[z], table_ref, 1, depth)


def solve(field, conductivity, rate):
    depth, cells_x, cells_y = field.shape
    rows, lanes = cells_x + 4 * MARGIN, cells_y
    arrays = (field, conductivity, rate)
    first = jnp.stack([x[:, :STEPS] for x in arrays])
    last = jnp.stack([x[:, cells_x - STEPS :] for x in arrays])
    below, above = exchange(first, last, "gx")
    halo = jnp.concatenate([below, above], 2)
    first, last = pack_sides(*arrays, halo)
    right, left = exchange(first, last, "gy")
    pos = [lax.axis_index("gx"), lax.axis_index("gy"), lax.axis_size("gx"), lax.axis_size("gy")]
    pos = jnp.stack([jnp.asarray(p, jnp.int32) for p in pos])
    padded = pltpu.VMEM((2, depth + 2, rows, lanes), jnp.float32)
    whole = pltpu.VMEM((2, depth, rows, lanes), jnp.float32)
    cells = cells_x * cells_y // PW
    return pl.pallas_call(
        solve_kernel,
        out_shape=(
            jax.ShapeDtypeStruct(field.shape, jnp.float32),
            jax.ShapeDtypeStruct((cells, 2 * depth * PW), jnp.bfloat16),
        ),
        in_specs=[pl.BlockSpec(memory_space=pltpu.SMEM)]
        + [pl.BlockSpec(memory_space=pltpu.VMEM)] * 6,
        out_specs=(pl.BlockSpec(memory_space=pltpu.VMEM),) * 2,
        scratch_shapes=[padded, padded, padded, whole, whole, whole,
            pltpu.VMEM((2, depth + 1, rows, lanes), jnp.float32),
            pltpu.VMEM((2, rows, lanes), jnp.float32)],
        cost_estimate=pl.CostEstimate(
            flops=80 * STEPS * depth * rows * lanes, bytes_accessed=64 << 20, transcendentals=0
        ),
        name="solve",
    )(pos, *arrays, halo, right, left)


def adam(param, moment, second, grad):
    moment_new = beta_one * moment + (1.0 - beta_one) * grad
    second_new = beta_two * second + (1.0 - beta_two) * grad * grad
    mhat = moment_new / (1.0 - beta_one**adam_count)
    vhat = second_new / (1.0 - beta_two**adam_count)
    return (param - learn_rate * mhat / (jnp.sqrt(vhat) + tiny_eps), moment_new, second_new)


def chip_groups(devices):
    return [list(range(core, devices, 2)) for core in range(2)]


def swap_cores(x, devices):
    return lax.ppermute(x, AXES, [(d, d ^ 1) for d in range(devices)])


def chips_all_to_all(x, devices):
    return lax.all_to_all(
        x, AXES, 0, 0, tiled=True, axis_index_groups=chip_groups(devices)
    )


def gather_params(weights, biases, hist, core, devices):
    chips = devices // 2
    layers, own, width = weights.shape
    extra = jnp.zeros((layers, own, devices), jnp.bfloat16)
    extra = extra.at[0, 0, :].set(hist.astype(jnp.bfloat16))
    extra = extra.at[:, 1, :own].set(biases.astype(jnp.bfloat16))
    pay = jnp.concatenate([weights.astype(jnp.bfloat16), extra], -1)
    got = chips_all_to_all(jnp.broadcast_to(pay[None], (chips,) + pay.shape), devices)
    other = swap_cores(got, devices)
    first = jnp.where(core == 0, got, other)
    second = jnp.where(core == 0, other, got)
    both = jnp.stack([first, second], 1).transpose(2, 0, 1, 3, 4)
    full = both.reshape(layers, devices * own, width + devices)
    tail = full[:, :, width:].reshape(layers, devices, own, devices)
    counts = jnp.sum(tail[0, :, 0, :].astype(jnp.float32), 0)
    bfull = tail[:, :, 1, :own].reshape(layers, devices * own).astype(jnp.float32)
    return full[:, :, :width], bfull, counts


def chunks(grad, devices):
    rows, width = grad.shape
    own = rows // devices
    tiles = width // 128
    grad = grad.reshape(devices // 2, 2, own, tiles, 128)
    return grad.transpose(1, 0, 3, 2, 4).reshape(2, devices // 2, tiles * own, 128)


def unchunk(share, own, width):
    return share.reshape(width // 128, own, 128).transpose(1, 0, 2).reshape(own, width)


def device_of(coords, core):
    z, x, y = coords
    return ((z * 4 + x) * 4 + y) * 2 + core


FAR_BIT = (6, 4, 2)


def halve(x, me, core, shifts, mask):
    bit = jnp.where(core == 0, me >> shifts[0], me >> shifts[1]) & 1
    keep = lax.dynamic_index_in_dim(x, bit, 0, keepdims=False)
    send = lax.dynamic_index_in_dim(x, 1 - bit, 0, keepdims=False)
    pairs = [(d, d ^ mask[d & 1]) for d in range(lax.axis_size(AXES))]
    return keep + lax.ppermute(send, AXES, pairs)


def axis_groups(axis, core):
    four = range(4)
    groups = []
    for p in four:
        places = [(q, r) for q in four for r in four]
        coords = [tuple(pair[:axis]) + (p,) + tuple(pair[axis:]) for pair in places]
        groups.append([device_of(c, core) for c in coords])
    return groups


def reduce_parts(parts, me, core, devices, axes):
    mine = lax.dynamic_index_in_dim(parts, core, 0, keepdims=False)
    theirs = lax.dynamic_index_in_dim(parts, 1 - core, 0, keepdims=False)
    theirs = swap_cores(theirs, devices)
    tile = parts.shape[2:]
    mine = (mine + theirs).reshape((4, 4, 4) + tile)
    turned = [jnp.moveaxis(mine, axis, 0) for axis in axes]
    mine = jnp.where(core == 0, *turned).reshape((2, 2, 16) + tile)
    far = [FAR_BIT[axis] for axis in axes]
    near = [bit - 1 for bit in far]
    mine = halve(mine, me, core, far, [3 << bit for bit in near])
    mine = halve(mine, me, core, near, [1 << bit for bit in near])
    groups = axis_groups(axes[0], 0) + axis_groups(axes[1], 1)
    got = lax.all_to_all(mine, AXES, 0, 0, tiled=True, axis_index_groups=groups)
    return jnp.sum(got, 0)


def step_all(
    field,
    conductivity,
    rate,
    patch_cell,
    trainer,
    res_slot,
    reservoir,
    weights,
    w_mom,
    w_var,
    biases,
    b_mom,
    b_var,
):
    _, cells_x, cells_y = field.shape
    devices = lax.axis_size("gx") * lax.axis_size("gy")
    me = lax.axis_index(AXES)
    core = me & 1
    own, width = weights.shape[1:]
    ids = jnp.arange(devices, dtype=jnp.int32)
    onehot = trainer == ids[None, :]
    hist = jnp.sum(onehot.astype(jnp.float32), 0)
    wfull, bfull, counts = gather_params(weights, biases, hist, core, devices)

    state, table = solve(field, conductivity, rate)
    blocks = cells_y // PW
    place = patch_cell % blocks * cells_x + patch_cell // blocks
    pick = place[:, None] == jnp.arange(table.shape[0], dtype=jnp.int32)[None, :]
    patches = jnp.dot(pick.astype(jnp.bfloat16), table, preferred_element_type=jnp.float32)
    patches = patches.astype(jnp.bfloat16)

    old = res_slot.shape[0]
    sizes = old + counts
    own_size = jnp.sum(jnp.where(ids == me, sizes, 0.0))
    new_size = jnp.sum(jnp.where(onehot, sizes[None, :], 0.0), 1)
    scale = 2.0 / jnp.concatenate([jnp.broadcast_to(own_size, (old,)), new_size])[:, None]
    stored = reservoir[res_slot]
    rows = jnp.concatenate([stored, patches], 0)

    inputs = rows[:, :width]
    target = rows[:, width:].astype(jnp.float32)
    pre = jnp.dot(inputs, wfull[0], preferred_element_type=jnp.float32) + bfull[0]
    hidden = lax.optimization_barrier(jnp.tanh(pre))
    hidden_b = hidden.astype(jnp.bfloat16)
    pred = jnp.dot(hidden_b, wfull[1], preferred_element_type=jnp.float32) + bfull[1]
    grad_pred = (pred - target) * scale
    grad_pred_b = grad_pred.astype(jnp.bfloat16)
    grad_w2 = jnp.dot(hidden_b.T, grad_pred_b, preferred_element_type=jnp.float32)
    share_w2 = reduce_parts(chunks(grad_w2, devices), me, core, devices, (0, 1))
    grad_hid = jnp.dot(grad_pred_b, wfull[1].T, preferred_element_type=jnp.float32)
    grad_pre = grad_hid * (1.0 - hidden * hidden)
    grad_pre_b = grad_pre.astype(jnp.bfloat16)
    grad_b0 = jnp.sum(grad_pre, 0)
    grad_w1 = jnp.dot(inputs.T, grad_pre_b, preferred_element_type=jnp.float32)
    grad_b = jnp.stack([grad_b0, jnp.sum(grad_pred, 0)])
    tile_b = grad_b.reshape(2, devices // 2, 2, own).transpose(2, 1, 0, 3)
    tile_b = jnp.pad(tile_b, ((0, 0), (0, 0), (0, 8 - 2), (0, 128 - own)))
    parts = jnp.concatenate([chunks(grad_w1, devices), tile_b], 2)
    share_w1 = reduce_parts(parts, me, core, devices, (1, 2))
    share_w = jnp.stack(
        [unchunk(share_w1[: own * width // 128], own, width), unchunk(share_w2, own, width)]
    )
    share_b = share_w1[own * width // 128 :][:2, :own]
    new_w, new_wm, new_wv = adam(weights, w_mom, w_var, share_w)
    new_b, new_bm, new_bv = adam(biases, b_mom, b_var, share_b)
    return (state, new_w, new_wm, new_wv, new_b, new_bm, new_bv)


def solution(mesh):
    return jax.shard_map(
        step_all,
        mesh=mesh,
        in_specs=(
            P(None, "gx", "gy"),
            P(None, "gx", "gy"),
            P(None, "gx", "gy"),
            P(("gx", "gy")),
            P(("gx", "gy"), None),
            P(("gx", "gy")),
            P(("gx", "gy"), None),
            P(None, ("gx", "gy"), None),
            P(None, ("gx", "gy"), None),
            P(None, ("gx", "gy"), None),
            P(None, ("gx", "gy")),
            P(None, ("gx", "gy")),
            P(None, ("gx", "gy")),
        ),
        out_specs=(
            P(None, "gx", "gy"),
            P(None, ("gx", "gy"), None),
            P(None, ("gx", "gy"), None),
            P(None, ("gx", "gy"), None),
            P(None, ("gx", "gy")),
            P(None, ("gx", "gy")),
            P(None, ("gx", "gy")),
        ),
        check_vma=False,
    )
```

```python
import jax
import jax.numpy as jnp
from jax import lax
from jax.experimental import pallas as pl
from jax.experimental.pallas import tpu as pltpu
from jax.sharding import PartitionSpec as P


PW = 32
STEPS = 4
AXES = ("gx", "gy")

time_step = 0.15
learn_rate = 0.001
beta_one = 0.9
beta_two = 0.99
adam_count = 20
tiny_eps = 1e-08


def shift_pairs(axis):
    peers = lax.axis_size(axis)
    up = [(i, i + 1) for i in range(peers - 1)]
    return up, [(j, i) for i, j in up]


def exchange(first, last, axis):
    up, down = shift_pairs(axis)
    return lax.ppermute(first, axis, down), lax.ppermute(last, axis, up)


def lane_ids(shape):
    return lax.broadcasted_iota(jnp.int32, shape, len(shape) - 1)


def pack_kernel(u_ref, k_ref, r_ref, halo_ref, first_ref, last_ref):
    depth = u_ref.shape[0]
    slot = lane_ids((1, 128)) // STEPS
    for a, ref in enumerate((u_ref, k_ref, r_ref)):
        for part, rows in (("main", ref.shape[1]), ("halo", 2 * STEPS)):
            first = jnp.zeros((rows, 128), jnp.float32)
            last = first
            for z in range(depth):
                slab = ref[z] if part == "main" else halo_ref[a, z]
                turned = pltpu.roll(slab, z * STEPS, 1) if z else slab
                first = jnp.where(slot == z, turned, first)
                last = jnp.where(slot == (z - 1) % depth, turned, last)
            at = slice(0, rows) if part == "main" else slice(ref.shape[1], ref.shape[1] + rows)
            first_ref[a, at, :] = first
            last_ref[a, at, :] = last


def pack_sides(field, conductivity, rate, halo):
    rows = field.shape[1] + 2 * STEPS
    out = jax.ShapeDtypeStruct((3, rows, 128), jnp.float32)
    return pl.pallas_call(pack_kernel, out_shape=(out, out), name="pack_sides", cost_estimate=pl.CostEstimate(flops=1 << 24, bytes_accessed=12 << 20, transcendentals=0))(
        field, conductivity, rate, halo
    )


def table_rows(read, table_ref, level, depth):
    group = lane_ids((1, 128)) // PW
    per = 128 // PW

    def body(block, carry):
        slabs = [read(block * per + k) for k in range(per)]
        cells_x = slabs[0].shape[0]
        for yb in range(per):
            row = None
            for k in range(per):
                turn = (k - yb) % per * PW
                part = pltpu.roll(slabs[k], turn, 1) if turn else slabs[k]
                row = part if row is None else jnp.where(group == k, part, row)
            at = pl.multiple_of(level * depth * PW + block * 128, 128)
            table_ref[yb * cells_x : (yb + 1) * cells_x, pl.ds(at, 128)] = row.astype(jnp.bfloat16)
        return carry

    lax.fori_loop(0, depth // per, body, 0, unroll=UNROLL)


MARGIN = 8
UNROLL = 4


def solve_kernel(
    pos_ref,
    u_ref,
    k_ref,
    r_ref,
    halo_ref,
    right_ref,
    left_ref,
    out_ref,
    table_ref,
    ua,
    ub,
    kk,
    rr,
    cx,
    cy,
    cl,
    cz,
    dt_ref,
):
    depth, cells_x, cells_y = u_ref.shape
    halo_top, main = MARGIN, 2 * MARGIN
    halo_low, end = main + cells_x, main + cells_x + MARGIN
    lane = lane_ids((1, cells_y))
    sub = lax.broadcasted_iota(jnp.int32, (8, cells_y), 0)
    col = lax.broadcasted_iota(jnp.int32, (8, cells_y), 1)
    blank = jnp.zeros((end + MARGIN, cells_y), jnp.float32)
    edge = jnp.zeros((MARGIN, cells_y), jnp.float32)
    for w in range(2):
        for ref in (ua, ub, kk):
            ref[w, 0] = blank
            ref[w, depth + 1] = blank

    def clear(z, carry):
        for w in range(2):
            for ref in (ua, ub, kk):
                ref[w, z + 1, 0:halo_top, :] = edge
                ref[w, z + 1, end : end + MARGIN, :] = edge
        return carry

    lax.fori_loop(0, depth, clear, 0)

    def place(ref, w, at, body, ends):
        ref[w, at, main:halo_low, :] = body
        ref[w, at, halo_top:main, :] = jnp.where(sub >= STEPS, ends, 0.0)
        ref[w, at, halo_low:end, :] = jnp.where(sub < STEPS, ends, 0.0)

    for z in range(depth):
        for a, (src, dst, at) in enumerate(((u_ref, ua, z + 1), (k_ref, kk, z + 1), (r_ref, rr, z))):
            place(dst, 0, at, src[z], halo_ref[a, z])
            turn = -z * STEPS % cells_y
            side = jnp.where(lane // STEPS == z, right_ref[a], left_ref[a])
            if turn:
                side = pltpu.roll(side, turn, 1)
            place(dst, 1, at, side[:cells_x], side[cells_x:])

    def rows(t, shift=0):
        return slice(8 * t + shift, 8 * t + 8 + shift)

    def turned(pair, back):
        amount = 1 if back else cells_y - 1
        seam = col == (0 if back else cells_y - 1)
        both = [pltpu.roll(x, amount, 1) for x in pair]
        return [jnp.where(seam, both[1 - w], both[w]) for w in range(2)]

    tiles = end // 8
    half = 0.5 * time_step

    def faces(z, carry):
        for t in range(tiles):
            k = [kk[w, z + 1, rows(t), :] for w in range(2)]
            after = turned(k, False)
            before = turned(k, True)
            for w in range(2):
                ahead = half * (k[w] + kk[w, z + 1, rows(t, 1), :])
                cx[w, z, rows(t), :] = ahead
                if t == 0:
                    continue
                low = half * (kk[w, z, rows(t), :] + k[w])
                cz[w, z, rows(t), :] = low
                right = half * (k[w] + after[w])
                left = half * (k[w] + before[w])
                cy[w, z, rows(t), :] = right
                cl[w, z, rows(t), :] = left
                loss = low + half * (k[w] + kk[w, z + 2, rows(t), :])
                loss = loss + (ahead + half * (k[w] + kk[w, z + 1, rows(t, -1), :]))
                loss = loss + (right + left)
                rr[w, z, rows(t), :] = (1.0 - time_step * rr[w, z, rows(t), :]) - loss
        return carry

    lax.fori_loop(0, depth, faces, 0, unroll=UNROLL)
    for w in range(2):
        cz[w, depth] = half * kk[w, depth]

    gx, gy = pos_ref[0], pos_ref[1]
    below = jnp.where(gx < pos_ref[2] - 1, 1, 0)
    above = jnp.where(gx > 0, 1, 0)
    after = jnp.where(gy < pos_ref[3] - 1, 1, 0)
    before = jnp.where(gy > 0, 1, 0)
    row_id = lax.broadcasted_iota(jnp.int32, blank.shape, 0)
    lane_id = lax.broadcasted_iota(jnp.int32, blank.shape, 1)
    row_in = jnp.where(row_id < main, above, jnp.where(row_id < halo_low, 1, below))
    row_in = jnp.where((row_id < main - STEPS) | (row_id >= halo_low + STEPS), 0, row_in)
    side_in = jnp.where(lane_id < STEPS, after, 0)
    side_in = jnp.where(lane_id >= cells_y - STEPS, before, side_in)
    for w, inside in ((0, row_in), (1, row_in * side_in)):
        dt_ref[w] = jnp.where(inside > 0, jnp.float32(1.0), jnp.float32(0.0))

    def advance(src, dst, last):
        picks = (0,) if last else (0, 1)
        first_tile, end_tile = (main // 8, halo_low // 8) if last else (halo_top // 8, end // 8)

        def body(z, carry):
            for t in range(first_tile, end_tile):
                u = [src[w, z + 1, rows(t), :] for w in range(2)]
                after = turned(u, False)
                before = turned(u, True)
                for w in picks:
                    total = cz[w, z + 1, rows(t), :] * src[w, z + 2, rows(t), :]
                    total = total + cz[w, z, rows(t), :] * src[w, z, rows(t), :]
                    total = total + cx[w, z, rows(t), :] * src[w, z + 1, rows(t, 1), :]
                    total = total + cx[w, z, rows(t, -1), :] * src[w, z + 1, rows(t, -1), :]
                    total = total + cy[w, z, rows(t), :] * after[w]
                    total = total + cl[w, z, rows(t), :] * before[w]
                    total = total + rr[w, z, rows(t), :] * u[w]
                    if last:
                        out_ref[z, rows(t - main // 8), :] = total
                    elif w == 0 and main <= 8 * t < halo_low:
                        dst[w, z + 1, rows(t), :] = total
                    else:
                        dst[w, z + 1, rows(t), :] = dt_ref[w, rows(t), :] * total
            return carry

        lax.fori_loop(0, depth, body, 0, unroll=UNROLL)

    src, dst = ua, ub
    for step in range(STEPS):
        advance(src, dst, step == STEPS - 1)
        src, dst = dst, src
    table_rows(lambda z: u_ref[z], table_ref, 0, depth)
    table_rows(lambda z: out_ref[z], table_ref, 1, depth)


def solve(field, conductivity, rate):
    depth, cells_x, cells_y = field.shape
    rows, lanes = cells_x + 4 * MARGIN, cells_y
    arrays = (field, conductivity, rate)
    first = jnp.stack([x[:, :STEPS] for x in arrays])
    last = jnp.stack([x[:, cells_x - STEPS :] for x in arrays])
    below, above = exchange(first, last, "gx")
    halo = jnp.concatenate([below, above], 2)
    first, last = pack_sides(*arrays, halo)
    right, left = exchange(first, last, "gy")
    pos = [lax.axis_index("gx"), lax.axis_index("gy"), lax.axis_size("gx"), lax.axis_size("gy")]
    pos = jnp.stack([jnp.asarray(p, jnp.int32) for p in pos])
    padded = pltpu.VMEM((2, depth + 2, rows, lanes), jnp.float32)
    whole = pltpu.VMEM((2, depth, rows, lanes), jnp.float32)
    cells = cells_x * cells_y // PW
    return pl.pallas_call(
        solve_kernel,
        out_shape=(
            jax.ShapeDtypeStruct(field.shape, jnp.float32),
            jax.ShapeDtypeStruct((cells, 2 * depth * PW), jnp.bfloat16),
        ),
        in_specs=[pl.BlockSpec(memory_space=pltpu.SMEM)]
        + [pl.BlockSpec(memory_space=pltpu.VMEM)] * 6,
        out_specs=(pl.BlockSpec(memory_space=pltpu.VMEM),) * 2,
        scratch_shapes=[padded, padded, padded, whole, whole, whole, whole,
            pltpu.VMEM((2, depth + 1, rows, lanes), jnp.float32),
            pltpu.VMEM((2, rows, lanes), jnp.float32)],
        cost_estimate=pl.CostEstimate(
            flops=80 * STEPS * depth * rows * lanes, bytes_accessed=64 << 20, transcendentals=0
        ),
        name="solve",
    )(pos, *arrays, halo, right, left)


def adam(param, moment, second, grad):
    moment_new = beta_one * moment + (1.0 - beta_one) * grad
    second_new = beta_two * second + (1.0 - beta_two) * grad * grad
    mhat = moment_new / (1.0 - beta_one**adam_count)
    vhat = second_new / (1.0 - beta_two**adam_count)
    return (param - learn_rate * mhat / (jnp.sqrt(vhat) + tiny_eps), moment_new, second_new)


def chip_groups(devices):
    return [list(range(core, devices, 2)) for core in range(2)]


def swap_cores(x, devices):
    return lax.ppermute(x, AXES, [(d, d ^ 1) for d in range(devices)])


def chips_all_to_all(x, devices):
    return lax.all_to_all(
        x, AXES, 0, 0, tiled=True, axis_index_groups=chip_groups(devices)
    )


def gather_params(weights, biases, hist, core, devices):
    chips = devices // 2
    layers, own, width = weights.shape
    extra = jnp.zeros((layers, own, devices), jnp.bfloat16)
    extra = extra.at[0, 0, :].set(hist.astype(jnp.bfloat16))
    extra = extra.at[:, 1, :own].set(biases.astype(jnp.bfloat16))
    pay = jnp.concatenate([weights.astype(jnp.bfloat16), extra], -1)
    got = chips_all_to_all(jnp.broadcast_to(pay[None], (chips,) + pay.shape), devices)
    other = swap_cores(got, devices)
    first = jnp.where(core == 0, got, other)
    second = jnp.where(core == 0, other, got)
    both = jnp.stack([first, second], 1).transpose(2, 0, 1, 3, 4)
    full = both.reshape(layers, devices * own, width + devices)
    tail = full[:, :, width:].reshape(layers, devices, own, devices)
    counts = jnp.sum(tail[0, :, 0, :].astype(jnp.float32), 0)
    bfull = tail[:, :, 1, :own].reshape(layers, devices * own).astype(jnp.float32)
    return full[:, :, :width], bfull, counts


def chunks(grad, devices):
    rows, width = grad.shape
    own = rows // devices
    tiles = width // 128
    grad = grad.reshape(devices // 2, 2, own, tiles, 128)
    return grad.transpose(1, 0, 3, 2, 4).reshape(2, devices // 2, tiles * own, 128)


def unchunk(share, own, width):
    return share.reshape(width // 128, own, 128).transpose(1, 0, 2).reshape(own, width)


def device_of(coords, core):
    z, x, y = coords
    return ((z * 4 + x) * 4 + y) * 2 + core


FAR_BIT = (6, 4, 2)


def halve(x, me, core, shifts, mask):
    bit = jnp.where(core == 0, me >> shifts[0], me >> shifts[1]) & 1
    keep = lax.dynamic_index_in_dim(x, bit, 0, keepdims=False)
    send = lax.dynamic_index_in_dim(x, 1 - bit, 0, keepdims=False)
    pairs = [(d, d ^ mask[d & 1]) for d in range(lax.axis_size(AXES))]
    return keep + lax.ppermute(send, AXES, pairs)


def axis_groups(axis, core):
    four = range(4)
    groups = []
    for p in four:
        places = [(q, r) for q in four for r in four]
        coords = [tuple(pair[:axis]) + (p,) + tuple(pair[axis:]) for pair in places]
        groups.append([device_of(c, core) for c in coords])
    return groups


def reduce_parts(parts, me, core, devices, axes):
    mine = lax.dynamic_index_in_dim(parts, core, 0, keepdims=False)
    theirs = lax.dynamic_index_in_dim(parts, 1 - core, 0, keepdims=False)
    theirs = swap_cores(theirs, devices)
    tile = parts.shape[2:]
    mine = (mine + theirs).reshape((4, 4, 4) + tile)
    turned = [jnp.moveaxis(mine, axis, 0) for axis in axes]
    mine = jnp.where(core == 0, *turned).reshape((2, 2, 16) + tile)
    far = [FAR_BIT[axis] for axis in axes]
    near = [bit - 1 for bit in far]
    mine = halve(mine, me, core, far, [3 << bit for bit in near])
    mine = halve(mine, me, core, near, [1 << bit for bit in near])
    groups = axis_groups(axes[0], 0) + axis_groups(axes[1], 1)
    got = lax.all_to_all(mine, AXES, 0, 0, tiled=True, axis_index_groups=groups)
    return jnp.sum(got, 0)


def step_all(
    field,
    conductivity,
    rate,
    patch_cell,
    trainer,
    res_slot,
    reservoir,
    weights,
    w_mom,
    w_var,
    biases,
    b_mom,
    b_var,
):
    _, cells_x, cells_y = field.shape
    devices = lax.axis_size("gx") * lax.axis_size("gy")
    me = lax.axis_index(AXES)
    core = me & 1
    own, width = weights.shape[1:]
    ids = jnp.arange(devices, dtype=jnp.int32)
    onehot = trainer == ids[None, :]
    hist = jnp.sum(onehot.astype(jnp.float32), 0)
    wfull, bfull, counts = gather_params(weights, biases, hist, core, devices)

    state, table = solve(field, conductivity, rate)
    blocks = cells_y // PW
    place = patch_cell % blocks * cells_x + patch_cell // blocks
    pick = place[:, None] == jnp.arange(table.shape[0], dtype=jnp.int32)[None, :]
    patches = jnp.dot(pick.astype(jnp.bfloat16), table, preferred_element_type=jnp.float32)
    patches = patches.astype(jnp.bfloat16)

    old = res_slot.shape[0]
    sizes = old + counts
    own_size = jnp.sum(jnp.where(ids == me, sizes, 0.0))
    new_size = jnp.sum(jnp.where(onehot, sizes[None, :], 0.0), 1)
    scale = 2.0 / jnp.concatenate([jnp.broadcast_to(own_size, (old,)), new_size])[:, None]
    stored = reservoir[res_slot]
    rows = jnp.concatenate([stored, patches], 0)

    inputs = rows[:, :width]
    target = rows[:, width:].astype(jnp.float32)
    pre = jnp.dot(inputs, wfull[0], preferred_element_type=jnp.float32) + bfull[0]
    hidden = lax.optimization_barrier(jnp.tanh(pre))
    hidden_b = hidden.astype(jnp.bfloat16)
    pred = jnp.dot(hidden_b, wfull[1], preferred_element_type=jnp.float32) + bfull[1]
    grad_pred = (pred - target) * scale
    grad_pred_b = grad_pred.astype(jnp.bfloat16)
    grad_w2 = jnp.dot(hidden_b.T, grad_pred_b, preferred_element_type=jnp.float32)
    share_w2 = reduce_parts(chunks(grad_w2, devices), me, core, devices, (0, 1))
    grad_hid = jnp.dot(grad_pred_b, wfull[1].T, preferred_element_type=jnp.float32)
    grad_pre = grad_hid * (1.0 - hidden * hidden)
    grad_pre_b = grad_pre.astype(jnp.bfloat16)
    grad_b0 = jnp.sum(grad_pre, 0)
    grad_w1 = jnp.dot(inputs.T, grad_pre_b, preferred_element_type=jnp.float32)
    grad_b = jnp.stack([grad_b0, jnp.sum(grad_pred, 0)])
    tile_b = grad_b.reshape(2, devices // 2, 2, own).transpose(2, 1, 0, 3)
    tile_b = jnp.pad(tile_b, ((0, 0), (0, 0), (0, 8 - 2), (0, 128 - own)))
    parts = jnp.concatenate([chunks(grad_w1, devices), tile_b], 2)
    share_w1 = reduce_parts(parts, me, core, devices, (1, 2))
    share_w = jnp.stack(
        [unchunk(share_w1[: own * width // 128], own, width), unchunk(share_w2, own, width)]
    )
    share_b = share_w1[own * width // 128 :][:2, :own]
    new_w, new_wm, new_wv = adam(weights, w_mom, w_var, share_w)
    new_b, new_bm, new_bv = adam(biases, b_mom, b_var, share_b)
    return (state, new_w, new_wm, new_wv, new_b, new_bm, new_bv)


def solution(mesh):
    return jax.shard_map(
        step_all,
        mesh=mesh,
        in_specs=(
            P(None, "gx", "gy"),
            P(None, "gx", "gy"),
            P(None, "gx", "gy"),
            P(("gx", "gy")),
            P(("gx", "gy"), None),
            P(("gx", "gy")),
            P(("gx", "gy"), None),
            P(None, ("gx", "gy"), None),
            P(None, ("gx", "gy"), None),
            P(None, ("gx", "gy"), None),
            P(None, ("gx", "gy")),
            P(None, ("gx", "gy")),
            P(None, ("gx", "gy")),
        ),
        out_specs=(
            P(None, "gx", "gy"),
            P(None, ("gx", "gy"), None),
            P(None, ("gx", "gy"), None),
            P(None, ("gx", "gy"), None),
            P(None, ("gx", "gy")),
            P(None, ("gx", "gy")),
            P(None, ("gx", "gy")),
        ),
        check_vma=False,
    )
```

```python
import jax
import jax.numpy as jnp
from jax import lax
from jax.experimental import pallas as pl
from jax.experimental.pallas import tpu as pltpu
from jax.sharding import PartitionSpec as P


PW = 32
STEPS = 4
AXES = ("gx", "gy")

time_step = 0.15
learn_rate = 0.001
beta_one = 0.9
beta_two = 0.99
adam_count = 20
tiny_eps = 1e-08


def shift_pairs(axis):
    peers = lax.axis_size(axis)
    up = [(i, i + 1) for i in range(peers - 1)]
    return up, [(j, i) for i, j in up]


def exchange(first, last, axis):
    up, down = shift_pairs(axis)
    return lax.ppermute(first, axis, down), lax.ppermute(last, axis, up)


def lane_ids(shape):
    return lax.broadcasted_iota(jnp.int32, shape, len(shape) - 1)


def pack_kernel(u_ref, k_ref, r_ref, halo_ref, first_ref, last_ref):
    depth = u_ref.shape[0]
    slot = lane_ids((1, 128)) // STEPS
    for a, ref in enumerate((u_ref, k_ref, r_ref)):
        for part, rows in (("main", ref.shape[1]), ("halo", 2 * STEPS)):
            first = jnp.zeros((rows, 128), jnp.float32)
            last = first
            for z in range(depth):
                slab = ref[z] if part == "main" else halo_ref[a, z]
                turned = pltpu.roll(slab, z * STEPS, 1) if z else slab
                first = jnp.where(slot == z, turned, first)
                last = jnp.where(slot == (z - 1) % depth, turned, last)
            at = slice(0, rows) if part == "main" else slice(ref.shape[1], ref.shape[1] + rows)
            first_ref[a, at, :] = first
            last_ref[a, at, :] = last


def pack_sides(field, conductivity, rate, halo):
    rows = field.shape[1] + 2 * STEPS
    out = jax.ShapeDtypeStruct((3, rows, 128), jnp.float32)
    return pl.pallas_call(pack_kernel, out_shape=(out, out), name="pack_sides", cost_estimate=pl.CostEstimate(flops=1 << 24, bytes_accessed=12 << 20, transcendentals=0))(
        field, conductivity, rate, halo
    )


def table_rows(read, table_ref, level, depth):
    group = lane_ids((1, 128)) // PW
    per = 128 // PW

    def body(block, carry):
        slabs = [read(block * per + k) for k in range(per)]
        cells_x = slabs[0].shape[0]
        for yb in range(per):
            row = None
            for k in range(per):
                turn = (k - yb) % per * PW
                part = pltpu.roll(slabs[k], turn, 1) if turn else slabs[k]
                row = part if row is None else jnp.where(group == k, part, row)
            at = pl.multiple_of(level * depth * PW + block * 128, 128)
            table_ref[yb * cells_x : (yb + 1) * cells_x, pl.ds(at, 128)] = row.astype(jnp.bfloat16)
        return carry

    lax.fori_loop(0, depth // per, body, 0, unroll=UNROLL)


MARGIN = 8
UNROLL = 4


def solve_kernel(
    pos_ref,
    u_ref,
    k_ref,
    r_ref,
    halo_ref,
    right_ref,
    left_ref,
    out_ref,
    table_ref,
    ua,
    ub,
    kk,
    rr,
    cx,
    cy,
    cl,
    cz,
    dt_ref,
):
    depth, cells_x, cells_y = u_ref.shape
    halo_top, main = MARGIN, 2 * MARGIN
    halo_low, end = main + cells_x, main + cells_x + MARGIN
    lane = lane_ids((1, cells_y))
    sub = lax.broadcasted_iota(jnp.int32, (8, cells_y), 0)
    col = lax.broadcasted_iota(jnp.int32, (8, cells_y), 1)
    blank = jnp.zeros((end + MARGIN, cells_y), jnp.float32)
    edge = jnp.zeros((MARGIN, cells_y), jnp.float32)
    for w in range(2):
        for ref in (ua, ub, kk):
            ref[w, 0] = blank
            ref[w, depth + 1] = blank

    def clear(z, carry):
        for w in range(2):
            for ref in (ua, ub, kk):
                ref[w, z + 1, 0:halo_top, :] = edge
                ref[w, z + 1, end : end + MARGIN, :] = edge
        return carry

    lax.fori_loop(0, depth, clear, 0)

    def place(ref, w, at, body, ends):
        ref[w, at, main:halo_low, :] = body
        ref[w, at, halo_top:main, :] = jnp.where(sub >= STEPS, ends, 0.0)
        ref[w, at, halo_low:end, :] = jnp.where(sub < STEPS, ends, 0.0)

    for z in range(depth):
        for a, (src, dst, at) in enumerate(((u_ref, ua, z + 1), (k_ref, kk, z + 1), (r_ref, rr, z))):
            place(dst, 0, at, src[z], halo_ref[a, z])
            turn = -z * STEPS % cells_y
            side = jnp.where(lane // STEPS == z, right_ref[a], left_ref[a])
            if turn:
                side = pltpu.roll(side, turn, 1)
            place(dst, 1, at, side[:cells_x], side[cells_x:])

    def rows(t, shift=0):
        return slice(8 * t + shift, 8 * t + 8 + shift)

    def turned(pair, back):
        amount = 1 if back else cells_y - 1
        seam = col == (0 if back else cells_y - 1)
        both = [pltpu.roll(x, amount, 1) for x in pair]
        return [jnp.where(seam, both[1 - w], both[w]) for w in range(2)]

    tiles = end // 8
    half = 0.5 * time_step

    def faces(z, carry):
        for t in range(tiles):
            k = [kk[w, z + 1, rows(t), :] for w in range(2)]
            after = turned(k, False)
            before = turned(k, True)
            for w in range(2):
                ahead = half * (k[w] + kk[w, z + 1, rows(t, 1), :])
                cx[w, z, rows(t), :] = ahead
                if t == 0:
                    continue
                low = half * (kk[w, z, rows(t), :] + k[w])
                cz[w, z, rows(t), :] = low
                right = half * (k[w] + after[w])
                left = half * (k[w] + before[w])
                cy[w, z, rows(t), :] = right
                cl[w, z, rows(t), :] = left
                loss = low + half * (k[w] + kk[w, z + 2, rows(t), :])
                loss = loss + (ahead + half * (k[w] + kk[w, z + 1, rows(t, -1), :]))
                loss = loss + (right + left)
                rr[w, z, rows(t), :] = (1.0 - time_step * rr[w, z, rows(t), :]) - loss
        return carry

    lax.fori_loop(0, depth, faces, 0, unroll=UNROLL)
    for w in range(2):
        cz[w, depth] = half * kk[w, depth]

    gx, gy = pos_ref[0], pos_ref[1]
    below = jnp.where(gx < pos_ref[2] - 1, 1, 0)
    above = jnp.where(gx > 0, 1, 0)
    after = jnp.where(gy < pos_ref[3] - 1, 1, 0)
    before = jnp.where(gy > 0, 1, 0)
    row_id = lax.broadcasted_iota(jnp.int32, blank.shape, 0)
    lane_id = lax.broadcasted_iota(jnp.int32, blank.shape, 1)
    row_in = jnp.where(row_id < main, above, jnp.where(row_id < halo_low, 1, below))
    row_in = jnp.where((row_id < main - STEPS) | (row_id >= halo_low + STEPS), 0, row_in)
    side_in = jnp.where(lane_id < STEPS, after, 0)
    side_in = jnp.where(lane_id >= cells_y - STEPS, before, side_in)
    for w, inside in ((0, row_in), (1, row_in * side_in)):
        dt_ref[w] = jnp.where(inside > 0, jnp.float32(1.0), jnp.float32(0.0))

    def advance(src, dst, last):
        picks = (0,) if last else (0, 1)
        first_tile, end_tile = (main // 8, halo_low // 8) if last else (halo_top // 8, end // 8)

        def body(z, carry):
            for t in range(first_tile, end_tile):
                u = [src[w, z + 1, rows(t), :] for w in range(2)]
                after = turned(u, False)
                before = turned(u, True)
                for w in picks:
                    total = cz[w, z + 1, rows(t), :] * src[w, z + 2, rows(t), :]
                    total = total + cz[w, z, rows(t), :] * src[w, z, rows(t), :]
                    total = total + cx[w, z, rows(t), :] * src[w, z + 1, rows(t, 1), :]
                    total = total + cx[w, z, rows(t, -1), :] * src[w, z + 1, rows(t, -1), :]
                    total = total + cy[w, z, rows(t), :] * after[w]
                    total = total + cl[w, z, rows(t), :] * before[w]
                    total = total + rr[w, z, rows(t), :] * u[w]
                    if last:
                        out_ref[z, rows(t - main // 8), :] = total
                    elif w == 0 and main <= 8 * t < halo_low:
                        dst[w, z + 1, rows(t), :] = total
                    else:
                        dst[w, z + 1, rows(t), :] = dt_ref[w, rows(t), :] * total
            return carry

        lax.fori_loop(0, depth, body, 0, unroll=UNROLL)

    src, dst = ua, ub
    for step in range(STEPS):
        advance(src, dst, step == STEPS - 1)
        src, dst = dst, src
    table_rows(lambda z: u_ref[z], table_ref, 0, depth)
    table_rows(lambda z: out_ref[z], table_ref, 1, depth)


def solve(field, conductivity, rate):
    depth, cells_x, cells_y = field.shape
    rows, lanes = cells_x + 4 * MARGIN, cells_y
    arrays = (field, conductivity, rate)
    first = jnp.stack([x[:, :STEPS] for x in arrays])
    last = jnp.stack([x[:, cells_x - STEPS :] for x in arrays])
    below, above = exchange(first, last, "gx")
    halo = jnp.concatenate([below, above], 2)
    first, last = pack_sides(*arrays, halo)
    right, left = exchange(first, last, "gy")
    pos = [lax.axis_index("gx"), lax.axis_index("gy"), lax.axis_size("gx"), lax.axis_size("gy")]
    pos = jnp.stack([jnp.asarray(p, jnp.int32) for p in pos])
    padded = pltpu.VMEM((2, depth + 2, rows, lanes), jnp.float32)
    whole = pltpu.VMEM((2, depth, rows, lanes), jnp.float32)
    cells = cells_x * cells_y // PW
    return pl.pallas_call(
        solve_kernel,
        out_shape=(
            jax.ShapeDtypeStruct(field.shape, jnp.float32),
            jax.ShapeDtypeStruct((cells, 2 * depth * PW), jnp.bfloat16),
        ),
        in_specs=[pl.BlockSpec(memory_space=pltpu.SMEM)]
        + [pl.BlockSpec(memory_space=pltpu.VMEM)] * 6,
        out_specs=(pl.BlockSpec(memory_space=pltpu.VMEM),) * 2,
        scratch_shapes=[padded, padded, padded, whole, whole, whole, whole,
            pltpu.VMEM((2, depth + 1, rows, lanes), jnp.float32),
            pltpu.VMEM((2, rows, lanes), jnp.float32)],
        cost_estimate=pl.CostEstimate(
            flops=80 * STEPS * depth * rows * lanes, bytes_accessed=64 << 20, transcendentals=0
        ),
        name="solve",
    )(pos, *arrays, halo, right, left)


def adam(param, moment, second, grad):
    moment_new = beta_one * moment + (1.0 - beta_one) * grad
    second_new = beta_two * second + (1.0 - beta_two) * grad * grad
    mhat = moment_new / (1.0 - beta_one**adam_count)
    vhat = second_new / (1.0 - beta_two**adam_count)
    return (param - learn_rate * mhat / (jnp.sqrt(vhat) + tiny_eps), moment_new, second_new)


def chip_groups(devices):
    return [list(range(core, devices, 2)) for core in range(2)]


def swap_cores(x, devices):
    return lax.ppermute(x, AXES, [(d, d ^ 1) for d in range(devices)])


def chips_all_to_all(x, devices):
    return lax.all_to_all(
        x, AXES, 0, 0, tiled=True, axis_index_groups=chip_groups(devices)
    )


def gather_params(weights, biases, hist, core, devices):
    chips = devices // 2
    layers, own, width = weights.shape
    extra = jnp.zeros((layers, own, devices), jnp.bfloat16)
    extra = extra.at[0, 0, :].set(hist.astype(jnp.bfloat16))
    extra = extra.at[:, 1, :own].set(biases.astype(jnp.bfloat16))
    pay = jnp.concatenate([weights.astype(jnp.bfloat16), extra], -1)
    got = chips_all_to_all(jnp.broadcast_to(pay[None], (chips,) + pay.shape), devices)
    other = swap_cores(got, devices)
    first = jnp.where(core == 0, got, other)
    second = jnp.where(core == 0, other, got)
    both = jnp.stack([first, second], 1).transpose(2, 0, 1, 3, 4)
    full = both.reshape(layers, devices * own, width + devices)
    tail = full[:, :, width:].reshape(layers, devices, own, devices)
    counts = jnp.sum(tail[0, :, 0, :].astype(jnp.float32), 0)
    bfull = tail[:, :, 1, :own].reshape(layers, devices * own).astype(jnp.float32)
    return full[:, :, :width], bfull, counts


def chunks(grad, devices):
    rows, width = grad.shape
    own = rows // devices
    tiles = width // 128
    grad = grad.reshape(devices // 2, 2, own, tiles, 128)
    return grad.transpose(1, 0, 3, 2, 4).reshape(2, devices // 2, tiles * own, 128)


def unchunk(share, own, width):
    return share.reshape(width // 128, own, 128).transpose(1, 0, 2).reshape(own, width)


def device_of(coords, core):
    z, x, y = coords
    return ((z * 4 + x) * 4 + y) * 2 + core


FAR_BIT = (6, 4, 2)
TURNS = (0, 1)


def halve(x, me, core, shifts, mask):
    bit = jnp.where(core == 0, me >> shifts[0], me >> shifts[1]) & 1
    keep = lax.dynamic_index_in_dim(x, bit, 0, keepdims=False)
    send = lax.dynamic_index_in_dim(x, 1 - bit, 0, keepdims=False)
    pairs = [(d, d ^ mask[d & 1]) for d in range(lax.axis_size(AXES))]
    return keep + lax.ppermute(send, AXES, pairs)


def axis_groups(axis, core):
    four = range(4)
    groups = []
    for p in four:
        places = [(q, r) for q in four for r in four]
        coords = [tuple(pair[:axis]) + (p,) + tuple(pair[axis:]) for pair in places]
        groups.append([device_of(c, core) for c in coords])
    return groups


def reduce_parts(parts, me, core, devices, axes):
    mine = lax.dynamic_index_in_dim(parts, core, 0, keepdims=False)
    theirs = lax.dynamic_index_in_dim(parts, 1 - core, 0, keepdims=False)
    theirs = swap_cores(theirs, devices)
    tile = parts.shape[2:]
    mine = (mine + theirs).reshape((4, 4, 4) + tile)
    turned = [jnp.moveaxis(mine, axis, 0) for axis in axes]
    mine = jnp.where(core == 0, *turned).reshape((2, 2, 16) + tile)
    far = [FAR_BIT[axis] for axis in axes]
    near = [bit - 1 for bit in far]
    mine = halve(mine, me, core, far, [3 << bit for bit in near])
    mine = halve(mine, me, core, near, [1 << bit for bit in near])
    return mine


def spread(mine, axes):
    groups = axis_groups(axes[0], 0) + axis_groups(axes[1], 1)
    got = lax.all_to_all(mine, AXES, 0, 0, tiled=True, axis_index_groups=groups)
    return jnp.sum(got, 0)


def step_all(
    field,
    conductivity,
    rate,
    patch_cell,
    trainer,
    res_slot,
    reservoir,
    weights,
    w_mom,
    w_var,
    biases,
    b_mom,
    b_var,
):
    _, cells_x, cells_y = field.shape
    devices = lax.axis_size("gx") * lax.axis_size("gy")
    me = lax.axis_index(AXES)
    core = me & 1
    own, width = weights.shape[1:]
    ids = jnp.arange(devices, dtype=jnp.int32)
    onehot = trainer == ids[None, :]
    hist = jnp.sum(onehot.astype(jnp.float32), 0)
    wfull, bfull, counts = gather_params(weights, biases, hist, core, devices)

    state, table = solve(field, conductivity, rate)
    blocks = cells_y // PW
    place = patch_cell % blocks * cells_x + patch_cell // blocks
    pick = place[:, None] == jnp.arange(table.shape[0], dtype=jnp.int32)[None, :]
    patches = jnp.dot(pick.astype(jnp.bfloat16), table, preferred_element_type=jnp.float32)
    patches = patches.astype(jnp.bfloat16)

    old = res_slot.shape[0]
    sizes = old + counts
    own_size = jnp.sum(jnp.where(ids == me, sizes, 0.0))
    new_size = jnp.sum(jnp.where(onehot, sizes[None, :], 0.0), 1)
    scale = 2.0 / jnp.concatenate([jnp.broadcast_to(own_size, (old,)), new_size])[:, None]
    stored = reservoir[res_slot]
    rows = jnp.concatenate([stored, patches], 0)

    inputs = rows[:, :width]
    target = rows[:, width:].astype(jnp.float32)
    pre = jnp.dot(inputs, wfull[0], preferred_element_type=jnp.float32) + bfull[0]
    hidden = lax.optimization_barrier(jnp.tanh(pre))
    hidden_b = hidden.astype(jnp.bfloat16)
    pred = jnp.dot(hidden_b, wfull[1], preferred_element_type=jnp.float32) + bfull[1]
    grad_pred = (pred - target) * scale
    grad_pred_b = grad_pred.astype(jnp.bfloat16)
    grad_w2 = jnp.dot(hidden_b.T, grad_pred_b, preferred_element_type=jnp.float32)
    share_w2 = reduce_parts(chunks(grad_w2, devices), me, core, devices, TURNS)
    grad_hid = jnp.dot(grad_pred_b, wfull[1].T, preferred_element_type=jnp.float32)
    grad_pre = grad_hid * (1.0 - hidden * hidden)
    grad_pre_b = grad_pre.astype(jnp.bfloat16)
    grad_b0 = jnp.sum(grad_pre, 0)
    grad_w1 = jnp.dot(inputs.T, grad_pre_b, preferred_element_type=jnp.float32)
    grad_b = jnp.stack([grad_b0, jnp.sum(grad_pred, 0)])
    tile_b = grad_b.reshape(2, devices // 2, 2, own).transpose(2, 1, 0, 3)
    tile_b = jnp.pad(tile_b, ((0, 0), (0, 0), (0, 8 - 2), (0, 128 - own)))
    parts = jnp.concatenate([chunks(grad_w1, devices), tile_b], 2)
    share_w1 = reduce_parts(parts, me, core, devices, TURNS)
    share = spread(jnp.concatenate([share_w2, share_w1], 1), TURNS)
    share_w2, share_w1 = share[: own * width // 128], share[own * width // 128 :]
    share_w = jnp.stack(
        [unchunk(share_w1[: own * width // 128], own, width), unchunk(share_w2, own, width)]
    )
    share_b = share_w1[own * width // 128 :][:2, :own]
    new_w, new_wm, new_wv = adam(weights, w_mom, w_var, share_w)
    new_b, new_bm, new_bv = adam(biases, b_mom, b_var, share_b)
    return (state, new_w, new_wm, new_wv, new_b, new_bm, new_bv)


def solution(mesh):
    return jax.shard_map(
        step_all,
        mesh=mesh,
        in_specs=(
            P(None, "gx", "gy"),
            P(None, "gx", "gy"),
            P(None, "gx", "gy"),
            P(("gx", "gy")),
            P(("gx", "gy"), None),
            P(("gx", "gy")),
            P(("gx", "gy"), None),
            P(None, ("gx", "gy"), None),
            P(None, ("gx", "gy"), None),
            P(None, ("gx", "gy"), None),
            P(None, ("gx", "gy")),
            P(None, ("gx", "gy")),
            P(None, ("gx", "gy")),
        ),
        out_specs=(
            P(None, "gx", "gy"),
            P(None, ("gx", "gy"), None),
            P(None, ("gx", "gy"), None),
            P(None, ("gx", "gy"), None),
            P(None, ("gx", "gy")),
            P(None, ("gx", "gy")),
            P(None, ("gx", "gy")),
        ),
        check_vma=False,
    )
```
